256 devices in a mesh: gx: 8 (over x, z_hi), gy: 8 (over y, core), gz: 4 (over z_lo).
Axes of the slice: x: 4, y: 4, z: 8 (z_hi: 2, z_lo: 4; z = z_hi * 4 + z_lo), core: 2. Of those that a mesh axis runs over, the one named last changes fastest.
Arguments:
- features: bfloat16 [8, 8, 4, 512, 128], P('gx', 'gy', 'gz'), may hold values from -6 to 6
- positions: float32 [8, 8, 4, 3, 512], P('gx', 'gy', 'gz'), may hold values from 0 to 1
- counts: int32 [8, 8, 4], P('gx', 'gy', 'gz'), may hold values from 256 to 512, as said below
- pair_first: int32 [8, 8, 4, 128, 128], P('gx', 'gy', 'gz'), may hold values from 0 to 511, as said below
- pair_second: int32 [8, 8, 4, 128, 128], P('gx', 'gy', 'gz'), may hold values from 0 to 13823, as said below
- pair_mask: int32 [8, 8, 4, 128, 128], P('gx', 'gy', 'gz'), may hold values from 0 to 1, as said below
- w_centre: bfloat16 [128, 256], replicated, may hold values from -0.5 to 0.5
- w_neighbour: bfloat16 [128, 256], replicated, may hold values from -0.5 to 0.5
- w_charge: bfloat16 [128], replicated, may hold values from -0.5 to 0.5
- w_radial: float32 [8, 256], replicated, may hold values from -3.5 to 3.5
- w_hidden: bfloat16 [256, 256], replicated, may hold values from -0.375 to 0.375
- w_energy: float32 [256], replicated, may hold values from -0.375 to 0.375
Outputs:
- forces: float32 [8, 8, 4, 3, 512], P('gx', 'gy', 'gz')
- charge_grad: float32 [8, 8, 4, 512], P('gx', 'gy', 'gz')
The draws below stay inside these ranges and needn't reach their ends.
Inputs may be any that keep to these rules, and one draw needn't show every extreme that they name: `counts`: every brick holds at least half of its slots; some brick is full and some holds exactly half; the atoms present fill the lowest slots. `pair_first`: every listed pair names a present atom of its own brick. `pair_second`: every listed pair names a present atom of the image brick of its slot s (entry s * 512 + a); within slot 13 it differs from the pair's first atom. `pair_mask`: on every brick the tiles that hold a valid pair come before those that hold none; tile 0 always holds valid pairs.
All inputs are finite; a program needn't handle non-finite values.
Results may differ from the reference program's by a relative error of at most 0.0032.
Values may be sent and summed in bfloat16 or wider, within the bound.
No kernel may reach another device: no remote copies, remote signals or barrier semaphores. Data moves between devices by JAX's collectives and lax.ppermute only.
A program may use at most 64 MiB of HBM per device.

```python
import jax
import jax.numpy as jnp
from jax import lax

ATOMS = 512
FEAT = 128
HID = 256
RBF = 8
TILES = 128
BX = 8
BY = 8
BZ = 4


def brick_counts(key):
    bricks = BX * BY * BZ
    base_sizes = jax.random.randint(jax.random.fold_in(key, 11), (bricks,), ATOMS // 2, ATOMS + 1)
    chosen = jax.random.randint(jax.random.fold_in(key, 12), (), 0, bricks)
    second = (chosen + 1 + jax.random.randint(jax.random.fold_in(key, 13), (), 0, bricks - 1)) % bricks
    brick_ids = jnp.arange(bricks)
    base_sizes = jnp.where(brick_ids == chosen, ATOMS, base_sizes)
    base_sizes = jnp.where(brick_ids == second, ATOMS // 2, base_sizes)
    return base_sizes.astype(jnp.int32)


def draw_counts(key, part):
    return brick_counts(key).reshape(BX, BY, BZ)


def pair_tables(key):
    bricks = BX * BY * BZ
    sizes_all = brick_counts(key)
    brick_ids = jnp.arange(bricks)[:, None, None]
    coord_x = brick_ids // (BY * BZ)
    coord_y = brick_ids // BZ % BY
    coord_z = brick_ids % BZ
    tile_shape = (bricks, TILES, 128)
    slot_pick = jax.random.randint(jax.random.fold_in(key, 21), tile_shape, 0, 27)
    step_x = slot_pick // 9 - 1
    step_y = slot_pick // 3 % 3 - 1
    step_z = slot_pick % 3 - 1
    other_id = (coord_x + step_x) % BX * (BY * BZ) + (coord_y + step_y) % BY * BZ + (coord_z + step_z) % BZ
    own_size = sizes_all[brick_ids]
    other_size = sizes_all[other_id]
    first_pick = jax.random.randint(jax.random.fold_in(key, 22), tile_shape, 0, 1 << 30) % own_size
    second_draw = jax.random.randint(jax.random.fold_in(key, 23), tile_shape, 0, 1 << 30)
    self_atom = (first_pick + 1 + second_draw % (own_size - 1)) % own_size
    second_atom = jnp.where(slot_pick == 13, self_atom, second_draw % other_size)
    second = slot_pick * ATOMS + second_atom
    lane_id = jnp.arange(128)[None, None, :]
    tile_id = jnp.arange(TILES)[None, :, None]
    corner = (coord_x + 1) % BX * (BY * BZ) + (coord_y + 1) % BY * BZ + (coord_z + 1) % BZ
    head_zero = (tile_id == 0) & (lane_id == 0)
    head_one = (tile_id == 0) & (lane_id == 1)
    first_pick = jnp.where(head_zero, own_size - 1, jnp.where(head_one, 0, first_pick))
    second = jnp.where(head_zero, 26 * ATOMS + sizes_all[corner] - 1, jnp.where(head_one, 0, second))
    live_tiles = jax.random.randint(jax.random.fold_in(key, 24), (bricks,), TILES // 8, TILES + 1)
    full_brick = jax.random.randint(jax.random.fold_in(key, 25), (), 0, bricks)
    live_tiles = jnp.where(jnp.arange(bricks) == full_brick, TILES, live_tiles)
    lanes_on = (jax.random.randint(jax.random.fold_in(key, 26), tile_shape, 0, 8) != 0) | (lane_id < 2)
    mask_out = ((tile_id < live_tiles[:, None, None]) & lanes_on).astype(jnp.int32)
    final_shape = (BX, BY, BZ, TILES, 128)
    return (first_pick.astype(jnp.int32).reshape(final_shape), second.astype(jnp.int32).reshape(final_shape), mask_out.reshape(final_shape))


def draw_pair_first(key, part):
    return pair_tables(key)[0]


def draw_pair_second(key, part):
    return pair_tables(key)[1]


def draw_pair_mask(key, part):
    return pair_tables(key)[2]


def shard_levels(rng, dims, cuts, least, high):
    level, own = 1.0, jax.random.fold_in(rng, 6)
    for position, blocks in cuts:
        heights = jnp.exp(jax.random.uniform(jax.random.fold_in(own, position), (blocks,), jnp.float32, least / len(cuts), high / len(cuts)))
        level = level * jnp.repeat(heights, dims[position] // blocks).reshape([-1 if axis == position else 1 for axis in range(len(dims))])
    return level


def normal_values(own_key, shape, width, reach, shards=(), kind=jnp.bfloat16):
    entries = width * jax.random.normal(own_key, shape, jnp.float32)
    if shards:
        entries = entries * shard_levels(own_key, shape, shards, -0.22, 0.18)
    return jnp.clip(entries, -reach, reach).astype(kind)


def setup_inputs(seed: int = 0) -> dict:
    streams_of = jax.random.split(jax.random.key(seed), 13)
    features = normal_values(streams_of[0], (BX, BY, BZ, ATOMS, FEAT), 1.0, 6.0, ((0, 8), (1, 8), (2, 4)))
    positions = jnp.clip(1.0 * jax.random.uniform(streams_of[1], (BX, BY, BZ, 3, ATOMS), jnp.float32) ** shard_levels(streams_of[1], (BX, BY, BZ, 3, ATOMS), ((0, 8), (1, 8), (2, 4)), -0.2, 0.2), 0.0, 1.0)
    counts = draw_counts(jax.random.fold_in(streams_of[12], 71), 0)
    pair_first = draw_pair_first(jax.random.fold_in(streams_of[12], 71), 0)
    pair_second = draw_pair_second(jax.random.fold_in(streams_of[12], 71), 0)
    pair_mask = draw_pair_mask(jax.random.fold_in(streams_of[12], 71), 0)
    w_centre = normal_values(streams_of[6], (FEAT, HID), FEAT ** -0.5, 0.5)
    w_neighbour = normal_values(streams_of[7], (FEAT, HID), FEAT ** -0.5, 0.5)
    w_charge = normal_values(streams_of[8], (FEAT,), FEAT ** -0.5, 0.5)
    w_radial = normal_values(streams_of[9], (RBF, HID), 3 ** -0.5, 3.5, (), jnp.float32)
    w_hidden = normal_values(streams_of[10], (HID, HID), HID ** -0.5, 0.375)
    w_energy = normal_values(streams_of[11], (HID,), HID ** -0.5, 0.375, (), jnp.float32)
    return dict(features=features, positions=positions, counts=counts, pair_first=pair_first, pair_second=pair_second, pair_mask=pair_mask, w_centre=w_centre, w_neighbour=w_neighbour, w_charge=w_charge, w_radial=w_radial, w_hidden=w_hidden, w_energy=w_energy)


delta_sq = 0.04
spread = 0.3
coulomb = 0.2
root_pi = 1.7724538509055159
block_tiles = 8

def silu_parts(value):
    logistic = jax.nn.sigmoid(value)
    return (value * logistic, logistic * (1.0 + value * (1.0 - logistic)))

def shifted_coords(neighbours):
    steps_axis = jnp.arange(3, dtype=jnp.float32) - 1.0
    zero_grid = jnp.zeros((3, 3, 3), jnp.float32)
    shift_grid = jnp.stack([steps_axis[:, None, None] + zero_grid, steps_axis[None, :, None] + zero_grid, steps_axis[None, None, :] + zero_grid, zero_grid], axis=3)
    moved_grid = neighbours + shift_grid[..., None]
    return jnp.moveaxis(moved_grid, 3, 0).reshape(4, -1)

def pair_block(centre_proj, image_proj, coords_own, coords_all, pick_first, pick_second, pick_mask, w_radial, w_hidden, w_energy):
    rows_i = pick_first.reshape(-1)
    rows_j = pick_second.reshape(-1)
    weight = pick_mask.reshape(-1).astype(jnp.float32)
    place_i = coords_own[:3][:, rows_i]
    place_j = coords_all[:3][:, rows_j]
    charge_i = coords_own[3][rows_i]
    charge_j = coords_all[3][rows_j]
    separation = place_j - place_i
    dist_sq = lax.optimization_barrier(jnp.sum(separation * separation, axis=0)) + delta_sq
    distance = jnp.sqrt(dist_sq)
    centres = 0.25 + 0.3 * jnp.arange(w_radial.shape[0], dtype=jnp.float32)
    offset = distance[None, :] - centres[:, None]
    radial_basis = jnp.exp(-(offset / spread) * (offset / spread))
    radial = lax.dot_general(radial_basis, w_radial, (((0,), (0,)), ((), ())), precision=lax.Precision.HIGHEST)
    pre_one = centre_proj[rows_i].astype(jnp.float32) + image_proj[rows_j].astype(jnp.float32) + radial
    act_one, slope_one = silu_parts(pre_one)
    hidden = act_one.astype(jnp.bfloat16)
    pre_two = jnp.dot(hidden, w_hidden, preferred_element_type=jnp.float32)
    act_two, slope_two = silu_parts(pre_two)
    envelope = jnp.exp(-0.5 * dist_sq)
    readout = jnp.dot(act_two, w_energy, precision=lax.Precision.HIGHEST)
    back_two = (envelope[:, None] * w_energy[None, :] * slope_two).astype(jnp.bfloat16)
    back_one = lax.dot_general(back_two, w_hidden, (((1,), (1,)), ((), ())), preferred_element_type=jnp.float32) * slope_one
    back_basis = lax.dot_general(w_radial, back_one, (((1,), (1,)), ((), ())), precision=lax.Precision.HIGHEST)
    slope_nn = lax.optimization_barrier(jnp.sum(back_basis * radial_basis * (-2.0 * offset / (spread * spread)), axis=0)) - readout * distance * envelope
    screened = lax.erfc(distance)
    coulomb_pot = screened / distance
    slope_coul = -(2.0 / root_pi) * jnp.exp(-dist_sq) / distance - screened / dist_sq
    slope_all = weight * (slope_nn + coulomb * charge_i * charge_j * slope_coul)
    push_pair = separation * (slope_all / distance)[None, :]
    term_i = jnp.concatenate([push_pair, (weight * coulomb * charge_j * coulomb_pot)[None, :]], axis=0)
    term_j = jnp.concatenate([-push_pair, (weight * coulomb * charge_i * coulomb_pot)[None, :]], axis=0)
    return (rows_i, term_i, rows_j, term_j)

def brick_sum(centre_proj, image_proj, coords_own, coords_all, pair_first, pair_second, pair_mask, w_radial, w_hidden, w_energy, block_count):
    atom_slots = centre_proj.shape[0]

    def advance(index, summed):
        begin_row = index * block_tiles
        rows_i, term_i, rows_j, term_j = pair_block(centre_proj, image_proj, coords_own, coords_all, lax.dynamic_slice_in_dim(pair_first, begin_row, block_tiles, 0), lax.dynamic_slice_in_dim(pair_second, begin_row, block_tiles, 0), lax.dynamic_slice_in_dim(pair_mask, begin_row, block_tiles, 0), w_radial, w_hidden, w_energy)
        summed = summed.at[13, :, rows_i].add(term_i.T)
        summed = summed.at[rows_j // atom_slots, :, rows_j % atom_slots].add(term_j.T)
        return summed
    start_sum = jnp.zeros((27, 4, atom_slots), jnp.float32)
    return lax.fori_loop(0, block_count, advance, start_sum)

def reference(features, positions, counts, pair_first, pair_second, pair_mask, w_centre, w_neighbour, w_charge, w_radial, w_hidden, w_energy):
    raw_charge = jnp.dot(features, w_charge, preferred_element_type=jnp.float32)
    slot_index = jnp.arange(ATOMS, dtype=jnp.int32)
    alive_slot = slot_index[None, None, None, :] < counts[..., None]
    average = lax.optimization_barrier(jnp.sum(jnp.where(alive_slot, raw_charge, 0.0), axis=-1)) / counts.astype(jnp.float32)
    charges = jnp.where(alive_slot, raw_charge - average[..., None], 0.0)
    coords = jnp.concatenate([positions, charges[:, :, :, None, :]], axis=3)
    centre_all = jnp.dot(features, w_centre, preferred_element_type=jnp.float32).astype(jnp.bfloat16)
    image_all = jnp.dot(features, w_neighbour, preferred_element_type=jnp.float32).astype(jnp.bfloat16)
    three = jnp.arange(3, dtype=jnp.int32) - 1

    def per_brick(brick_id):
        coord_x = brick_id // (BY * BZ)
        coord_y = brick_id // BZ % BY
        coord_z = brick_id % BZ
        near_x = (coord_x + three) % BX
        near_y = (coord_y + three) % BY
        near_z = (coord_z + three) % BZ

        def beside_all(table_all):
            return jnp.take(jnp.take(jnp.take(table_all, near_x, axis=0), near_y, axis=1), near_z, axis=2)
        image_proj = beside_all(image_all).reshape(27 * ATOMS, HID)
        coords_all = shifted_coords(beside_all(coords))
        return brick_sum(centre_all[coord_x, coord_y, coord_z], image_proj, coords[coord_x, coord_y, coord_z], coords_all, pair_first[coord_x, coord_y, coord_z], pair_second[coord_x, coord_y, coord_z], pair_mask[coord_x, coord_y, coord_z], w_radial, w_hidden, w_energy, TILES // block_tiles)
    partial_all = lax.map(per_brick, jnp.arange(BX * BY * BZ, dtype=jnp.int32))
    partial_all = partial_all.reshape(BX, BY, BZ, 3, 3, 3, 4, ATOMS)
    summed = jnp.zeros((BX, BY, BZ, 4, ATOMS), jnp.float32)
    for step_x in range(3):
        for step_y in range(3):
            for step_z in range(3):
                summed = summed + jnp.roll(partial_all[:, :, :, step_x, step_y, step_z], (step_x - 1, step_y - 1, step_z - 1), axis=(0, 1, 2))
    return (summed[:, :, :, :3], summed[:, :, :, 3])
```

```python
import jax
import jax.numpy as jnp
from jax import lax
from jax.experimental import pallas as pl
from jax.experimental.pallas import tpu as pltpu
from jax.sharding import PartitionSpec as P

delta_sq = 0.04
spread = 0.3
coulomb = 0.2
root_pi = 1.7724538509055159
chunk = 256
macro_chunks = 4
macro = chunk * macro_chunks

erfc_p = (
    2.326819970068386e-2, -1.387039388740657e-1, 3.687424674597105e-1, -5.824733027278666e-1,
    6.210004621745983e-1, -4.944515323274145e-1, 3.404879937665872e-1, -2.741127028184656e-1,
    5.638259427386472e-1,
)
erfc_r = (
    -1.047766399936249e1, 1.297719955372516e1, -7.495518717768503e0, 2.921019019210786e0,
    -1.015265279202700e0, 4.218463358204948e-1, -2.820767439740514e-1, 5.641895067754075e-1,
)
erf_t = (
    7.853861353153693e-5, -8.010193625184903e-4, 5.188327685732524e-3, -2.685381193529856e-2,
    1.128358514861418e-1, -3.761262582423300e-1, 1.128379165726710e0,
)


def poly(x, coefficients):
    total = jnp.full_like(x, coefficients[0])
    for value in coefficients[1:]:
        total = total * x + value
    return total


def erfc_positive(x, exp_minus_sq):
    square = x * x
    inverse = 1.0 / square
    tail = exp_minus_sq / x * jnp.where(x < 2.0, poly(inverse, erfc_p), poly(inverse, erfc_r))
    return jnp.where(x < 1.0, 1.0 - x * poly(square, erf_t), tail)


def geometry_kernel(coords_ref, first_ref, second_ref, mask_ref, out_ref):
    rows = 32

    def group(index, carry):
        base = pl.multiple_of(index * rows, rows)
        first = first_ref[pl.ds(base, rows), :]
        second = second_ref[pl.ds(base, rows), :]
        weight = mask_ref[pl.ds(base, rows), :].astype(jnp.float32)
        lane_j = second & 127
        row_j = second >> 7
        lane_i = first & 127
        row_i = first >> 7

        def pick(row, lanes):
            wide = jnp.broadcast_to(row, (rows, 128))
            return jnp.take_along_axis(wide, lanes, axis=1, mode="promise_in_bounds")

        def scan(slot, found):
            block = coords_ref[pl.ds(pl.multiple_of(slot * 16, 16), 16), :]
            for part in range(4):
                hit = row_j == slot * 4 + part
                found = tuple(
                    jnp.where(hit, pick(block[c * 4 + part : c * 4 + part + 1], lane_j), found[c])
                    for c in range(4)
                )
            return found

        zeros = jnp.zeros((rows, 128), jnp.float32)
        place_j = lax.fori_loop(0, 27, scan, (zeros,) * 4)
        own = coords_ref[13 * 16 : 14 * 16, :]
        place_i = [zeros] * 4
        for part in range(4):
            hit = row_i == part
            for c in range(4):
                place_i[c] = jnp.where(
                    hit, pick(own[c * 4 + part : c * 4 + part + 1], lane_i), place_i[c]
                )
        slot = second >> 9
        step_x = (slot * 57) >> 9
        rest = slot - step_x * 9
        step_y = (rest * 11) >> 5
        step_z = rest - step_y * 3
        sep = [
            (place_j[c] + (step.astype(jnp.float32) - 1.0)) - place_i[c]
            for c, step in enumerate((step_x, step_y, step_z))
        ]
        dist_sq = sep[0] * sep[0] + sep[1] * sep[1] + sep[2] * sep[2] + delta_sq
        distance = jnp.sqrt(dist_sq)
        inverse = 1.0 / distance
        exp_minus = jnp.exp(-dist_sq)
        screened = erfc_positive(distance, exp_minus)
        potential = screened * inverse
        slope_coul = -(2.0 / root_pi) * exp_minus * inverse - screened / dist_sq
        envelope = jnp.exp(-0.5 * dist_sq)
        values = (
            sep[0],
            sep[1],
            sep[2],
            distance,
            weight * envelope * inverse,
            weight * coulomb * place_i[3] * place_j[3] * slope_coul * inverse,
            weight * coulomb * place_j[3] * potential,
            weight * coulomb * place_i[3] * potential,
            jnp.where(first < 256, first, 512).astype(jnp.float32),
            jnp.where(first < 256, 512, first - 256).astype(jnp.float32),
            (second & 255).astype(jnp.float32),
            (second >> 8).astype(jnp.float32),
        )
        for position, value in enumerate(values):
            out_ref[pl.ds(base, rows), position, :] = value
        return carry

    lax.fori_loop(0, 128 // rows, group, 0)
    out_ref[:, 12:16, :] = jnp.zeros((128, 4, 128), jnp.float32)


def geometry(coords, first, second, mask):
    return pl.pallas_call(
        geometry_kernel,
        out_shape=jax.ShapeDtypeStruct((128, 16, 128), jnp.float32),
        name="geometry",
    )(coords, first, second, mask)


def pair_kernel(
    blocks_ref,
    rows_ref,
    low_ref,
    mid_ref,
    high_ref,
    geo_ref,
    centre_ref,
    neighbour_ref,
    radial_ref,
    hidden_ref,
    hidden_t_ref,
    energy_ref,
    back_ref,
    out_low,
    out_mid,
    out_high,
    stage_ref,
    table_ref,
    gather_ref,
    iota_ref,
    hot_ref,
    term_ref,
    acc_i_ref,
    acc_j_ref,
    sems,
):
    copies = [
        pltpu.make_async_copy(source, stage_ref.at[k], sems.at[k])
        for k, source in enumerate((low_ref, mid_ref, high_ref))
    ]
    for copy in copies:
        copy.start()
    iota_ref[...] = lax.broadcasted_iota(jnp.int32, (256, 128), 0).astype(jnp.float32).astype(jnp.bfloat16)
    acc_i_ref[...] = jnp.zeros_like(acc_i_ref)
    acc_j_ref[...] = jnp.zeros_like(acc_j_ref)
    for k in range(3):
        copies[k].wait()

        def widen(step, carry, k=k):
            rows = pl.ds(pl.multiple_of(step * 128, 128), 128)
            table_ref[pl.ds(pl.multiple_of(k * 4608 + step * 128, 128), 128), :] = stage_ref[
                k, rows, :
            ].astype(jnp.float32)
            return carry

        lax.fori_loop(0, 36, widen, 0)

    def fetch(index):
        for p in range(chunk):
            row = rows_ref[index * 2 + p // 128, p % 128]
            gather_ref[pl.ds(p, 1), :] = table_ref[pl.ds(row, 1), :]

    def wide(row):
        return jnp.broadcast_to(row.astype(jnp.bfloat16), (256, chunk))

    def one_hot(row):
        iota = jnp.concatenate([iota_ref[...]] * (chunk // 128), axis=1)
        return jnp.where(
            iota == wide(row), jnp.ones((), jnp.bfloat16), jnp.zeros((), jnp.bfloat16)
        )

    def step(part, first_chunk):
        index = first_chunk + part
        lanes = pl.ds(pl.multiple_of(part * chunk, chunk), chunk)
        geo = jnp.concatenate([geo_ref[index * 2], geo_ref[index * 2 + 1]], axis=1)
        features = gather_ref[...].astype(jnp.bfloat16)
        fetch(jnp.minimum(index + 1, 63))
        distance = geo[3:4]
        offset = distance - (
            0.25 + 0.3 * lax.broadcasted_iota(jnp.int32, (8, chunk), 0).astype(jnp.float32)
        )
        basis = jnp.exp(-(offset / spread) * (offset / spread))
        basis_slope = basis * offset * (-2.0 / (spread * spread))
        top = basis.astype(jnp.bfloat16).astype(jnp.float32)
        basis_parts = jnp.concatenate([top, top, basis - top, jnp.zeros_like(top)], axis=0)
        hot_low = one_hot(geo[8:9])
        hot_high = one_hot(geo[9:10])
        hot_ref[0:256, lanes] = hot_low
        hot_ref[256:512, lanes] = hot_high
        half_one = (
            jnp.dot(centre_ref[:, 0:256], hot_low, preferred_element_type=jnp.float32)
            + jnp.dot(centre_ref[:, 256:512], hot_high, preferred_element_type=jnp.float32)
            + lax.dot_general(
                neighbour_ref[...],
                features,
                (((1,), (1,)), ((), ())),
                preferred_element_type=jnp.float32,
            )
            + jnp.dot(
                radial_ref[...],
                basis_parts.astype(jnp.bfloat16),
                preferred_element_type=jnp.float32,
            )
        )
        bend_one = jnp.tanh(half_one)
        gain_one = 1.0 + bend_one
        act_one = half_one * gain_one
        slope_one = gain_one + act_one * (1.0 - bend_one)
        half_two = jnp.dot(
            hidden_t_ref[...], act_one.astype(jnp.bfloat16), preferred_element_type=jnp.float32
        )
        bend_two = jnp.tanh(half_two)
        gain_two = 1.0 + bend_two
        act_two = half_two * gain_two
        slope_two = gain_two + act_two * (1.0 - bend_two)
        energy = jnp.concatenate([energy_ref[...]] * (chunk // 128), axis=1)
        readout = jnp.sum(act_two * energy, axis=0, keepdims=True)
        back_two = (slope_two * energy).astype(jnp.bfloat16)
        back_one = (
            jnp.dot(hidden_ref[...], back_two, preferred_element_type=jnp.float32) * slope_one
        )
        back_basis = jnp.dot(
            back_ref[...], back_one.astype(jnp.bfloat16), preferred_element_type=jnp.float32
        )
        total = jnp.sum(
            (back_basis[0:8] + back_basis[8:16]) * basis_slope, axis=0, keepdims=True
        ) - (readout * distance)
        push = geo[4:5] * total + geo[5:6]
        term_ref[0:3, lanes] = geo[0:3] * push
        term_ref[3:5, lanes] = geo[6:8]
        return first_chunk

    fetch(0)

    def block(index, carry):
        lax.fori_loop(0, macro_chunks, step, index * macro_chunks)
        terms = term_ref[...]
        push = terms[0:3]
        own = jnp.concatenate([push, terms[3:4], jnp.zeros((4, macro), jnp.float32)], axis=0)
        own_top = own.astype(jnp.bfloat16).astype(jnp.float32)
        own_parts = jnp.concatenate([own_top, own - own_top], axis=0).astype(jnp.bfloat16)
        acc_i_ref[...] += lax.dot_general(
            own_parts, hot_ref[...], (((1,), (1,)), ((), ())), preferred_element_type=jnp.float32
        )
        far = jnp.concatenate([-push, terms[4:5]], axis=0)
        far_top = far.astype(jnp.bfloat16)
        far_rest = (far - far_top.astype(jnp.float32)).astype(jnp.bfloat16)
        geo = jnp.concatenate([geo_ref[index * 2 * macro_chunks + k] for k in range(macro // 128)], axis=1)
        iota = jnp.concatenate([iota_ref[...]] * (macro // 128), axis=1)
        one = jnp.ones((), jnp.bfloat16)
        zero = jnp.zeros((), jnp.bfloat16)
        hot = jnp.where(
            iota == jnp.broadcast_to(geo[10:11].astype(jnp.bfloat16), (256, macro)), one, zero
        )
        block_hit = jnp.where(
            iota[0:64] == jnp.broadcast_to(geo[11:12].astype(jnp.bfloat16), (64, macro)), one, zero
        )
        spread_rows = jnp.concatenate(
            [
                block_hit * jnp.broadcast_to(part[c : c + 1], (64, macro))
                for c in range(4)
                for part in (far_top, far_rest)
            ],
            axis=0,
        )
        acc_j_ref[...] += lax.dot_general(
            spread_rows, hot, (((1,), (1,)), ((), ())), preferred_element_type=jnp.float32
        )
        return carry

    lax.fori_loop(0, blocks_ref[0], block, 0)
    acc_i = acc_i_ref[...]
    acc_i = acc_i[0:8] + acc_i[8:16]
    for c in range(4):
        plane = acc_j_ref[c * 128 : c * 128 + 64, :] + acc_j_ref[c * 128 + 64 : c * 128 + 128, :]
        for slot in range(27):
            step_x, step_y, step_z = slot // 9, slot // 3 % 3, slot % 3
            target = (out_low, out_mid, out_high)[step_y]
            for half in range(2):
                row = plane[slot * 2 + half : slot * 2 + half + 1]
                if slot == 13:
                    row = row + acc_i[c : c + 1, half * 256 : half * 256 + 256]
                target[step_z * 3 + step_x, c * 2 + half : c * 2 + half + 1, :] = row


def pair_sums(block_count, rows, low, mid, high, geo, weights):
    vmem = pl.BlockSpec(memory_space=pltpu.VMEM)
    smem = pl.BlockSpec(memory_space=pltpu.SMEM)
    far = pl.BlockSpec(memory_space=pl.ANY)
    out = jax.ShapeDtypeStruct((9, 8, 256), jnp.float32)
    return pl.pallas_call(
        pair_kernel,
        out_shape=(out, out, out),
        in_specs=[smem, smem, far, far, far, vmem] + [vmem] * 7,
        out_specs=(vmem, vmem, vmem),
        scratch_shapes=[
            pltpu.VMEM((3, 4608, 128), jnp.bfloat16),
            pltpu.VMEM((13824, 128), jnp.float32),
            pltpu.VMEM((chunk, 128), jnp.float32),
            pltpu.VMEM((256, 128), jnp.bfloat16),
            pltpu.VMEM((512, macro), jnp.bfloat16),
            pltpu.VMEM((8, macro), jnp.float32),
            pltpu.VMEM((16, 512), jnp.float32),
            pltpu.VMEM((512, 256), jnp.float32),
            pltpu.SemaphoreType.DMA((3,)),
        ],
        compiler_params=pltpu.CompilerParams(vmem_limit_bytes=48 * 1024 * 1024),
        name="pairs",
    )(block_count, rows, low, mid, high, geo, *weights)


def swap(block, axis):
    count = lax.axis_size(axis)
    forward = [(i, (i + 1) % count) for i in range(count)]
    backward = [(target, source) for source, target in forward]
    return lax.ppermute(block, axis, forward), lax.ppermute(block, axis, backward)


def split(value):
    top = lax.reduce_precision(value, 8, 7)
    return top, value - top


def indices(second_tab, mask_tab, atom_slots):
    slot = second_tab >> 9
    step_x = slot // 9
    step_y = slot // 3 % 3
    step_z = slot % 3
    rows = (step_y * 9 + step_z * 3 + step_x) * atom_slots + (second_tab & (atom_slots - 1))
    busy_tiles = jnp.sum(jnp.any(mask_tab != 0, axis=1).astype(jnp.int32))
    tiles = macro // 128
    block_count = ((busy_tiles + tiles - 1) // tiles).reshape(1)
    return block_count, rows


def arrange(own_feat, w_centre, w_neighbour, w_radial, w_hidden, w_energy):
    centre_t = jnp.dot(own_feat, w_centre, preferred_element_type=jnp.float32).astype(
        jnp.bfloat16
    ).T * jnp.bfloat16(0.5)
    half = jnp.bfloat16(0.5)
    radial_top, radial_rest = split(w_radial * 0.5)
    zero_rows = jnp.zeros_like(radial_top)
    radial_t = (
        jnp.concatenate([radial_top, radial_rest, radial_top, zero_rows], axis=0)
        .astype(jnp.bfloat16)
        .T
    )
    back = jnp.concatenate([radial_top, radial_rest], axis=0).astype(jnp.bfloat16)
    energy = jnp.broadcast_to(w_energy[:, None], (w_energy.shape[0], 128))
    return (
        centre_t,
        w_neighbour.T * half,
        radial_t,
        w_hidden * half,
        w_hidden.T * half,
        energy,
        back,
    )


def local(
    features,
    positions,
    counts,
    pair_first,
    pair_second,
    pair_mask,
    w_centre,
    w_neighbour,
    w_charge,
    w_radial,
    w_hidden,
    w_energy,
):
    own_feat = features[0, 0, 0]
    atom_slots = own_feat.shape[0]
    raw_charge = jnp.dot(own_feat, w_charge, preferred_element_type=jnp.float32)
    filled = counts[0, 0, 0]
    alive_slot = jnp.arange(atom_slots, dtype=jnp.int32) < filled
    average = jnp.sum(jnp.where(alive_slot, raw_charge, 0.0)) / filled.astype(jnp.float32)
    charges = jnp.where(alive_slot, raw_charge - average, 0.0)
    coords_own = jnp.concatenate([positions[0, 0, 0], charges[None, :]], axis=0).reshape(16, 128)

    def collect(block):
        low, high = swap(block, "gx")
        line = jnp.stack([low, block, high], axis=0)
        low, high = swap(line, "gz")
        plane = jnp.concatenate([low, line, high], axis=0)
        low, high = swap(plane, "gy")
        return low, plane, high

    near_coords = jnp.stack(collect(coords_own), axis=0)
    low, mid, high = [part.reshape(9 * atom_slots, -1) for part in collect(own_feat)]
    coords_all = (
        near_coords.reshape(3, 3, 3, 16, 128).transpose(2, 0, 1, 3, 4).reshape(27 * 16, 128)
    )
    first_tab = pair_first[0, 0, 0]
    second_tab = pair_second[0, 0, 0]
    mask_tab = pair_mask[0, 0, 0]
    geo = geometry(coords_all, first_tab, second_tab, mask_tab)

    block_count, rows = indices(second_tab, mask_tab, atom_slots)
    weights = arrange(own_feat, w_centre, w_neighbour, w_radial, w_hidden, w_energy)
    out_low, out_mid, out_high = pair_sums(block_count, rows, low, mid, high, geo, weights)

    def give(low, mid, high, axis):
        count = lax.axis_size(axis)
        forward = [(i, (i + 1) % count) for i in range(count)]
        backward = [(target, source) for source, target in forward]
        return mid + lax.ppermute(high, axis, forward) + lax.ppermute(low, axis, backward)

    plane = give(out_low, out_mid, out_high, "gy")
    line = give(plane[0:3], plane[3:6], plane[6:9], "gz")
    summed = give(line[0], line[1], line[2], "gx").reshape(4, atom_slots)
    return (summed[:3][None, None, None], summed[3][None, None, None])


def solution(mesh):
    placed = (
        P("gx", "gy", "gz", None, None),
        P("gx", "gy", "gz", None, None),
        P("gx", "gy", "gz"),
        P("gx", "gy", "gz", None, None),
        P("gx", "gy", "gz", None, None),
        P("gx", "gy", "gz", None, None),
        P(),
        P(),
        P(),
        P(),
        P(),
        P(),
    )
    return jax.shard_map(
        local,
        mesh=mesh,
        in_specs=placed,
        out_specs=(P("gx", "gy", "gz", None, None), P("gx", "gy", "gz", None)),
        check_vma=False,
    )
```

```python
import jax
import jax.numpy as jnp
from jax import lax
from jax.experimental import pallas as pl
from jax.experimental.pallas import tpu as pltpu
from jax.sharding import PartitionSpec as P

delta_sq = 0.04
spread = 0.3
coulomb = 0.2
root_pi = 1.7724538509055159
chunk = 256
macro_chunks = 2
macro = chunk * macro_chunks

erfc_p = (
    2.326819970068386e-2, -1.387039388740657e-1, 3.687424674597105e-1, -5.824733027278666e-1,
    6.210004621745983e-1, -4.944515323274145e-1, 3.404879937665872e-1, -2.741127028184656e-1,
    5.638259427386472e-1,
)
erfc_r = (
    -1.047766399936249e1, 1.297719955372516e1, -7.495518717768503e0, 2.921019019210786e0,
    -1.015265279202700e0, 4.218463358204948e-1, -2.820767439740514e-1, 5.641895067754075e-1,
)
erf_t = (
    7.853861353153693e-5, -8.010193625184903e-4, 5.188327685732524e-3, -2.685381193529856e-2,
    1.128358514861418e-1, -3.761262582423300e-1, 1.128379165726710e0,
)


def poly(x, coefficients):
    total = jnp.full_like(x, coefficients[0])
    for value in coefficients[1:]:
        total = total * x + value
    return total


def erfc_positive(x, exp_minus_sq):
    square = x * x
    inverse = 1.0 / square
    tail = exp_minus_sq / x * jnp.where(x < 2.0, poly(inverse, erfc_p), poly(inverse, erfc_r))
    return jnp.where(x < 1.0, 1.0 - x * poly(square, erf_t), tail)


def geometry_kernel(coords_ref, first_ref, second_ref, mask_ref, out_ref, place_ref, top_ref):
    rows = 32
    wide = 512
    coords = jnp.concatenate([coords_ref[:, 0:8, :], coords_ref[:, 8:16, :]], axis=2)
    coords = coords.reshape(216, 256)
    coords_top = coords.astype(jnp.bfloat16)
    top_ref[:, 0:256] = coords_top
    top_ref[:, 256:512] = (coords - coords_top.astype(jnp.float32)).astype(jnp.bfloat16)

    def locate(index, carry):
        second = jnp.concatenate(
            [second_ref[pl.ds(index * 4 + k, 1), :] for k in range(4)], axis=1
        )
        low = (second & 255).astype(jnp.float32).astype(jnp.bfloat16)
        high = jnp.broadcast_to(second >> 8, (8, wide))
        iota = lax.broadcasted_iota(jnp.int32, (256, wide), 0).astype(jnp.float32)
        hot = jnp.where(
            iota.astype(jnp.bfloat16) == jnp.broadcast_to(low, (256, wide)),
            jnp.ones((), jnp.bfloat16),
            jnp.zeros((), jnp.bfloat16),
        )
        found = jnp.dot(
            top_ref[...],
            jnp.concatenate([hot, hot], axis=0),
            preferred_element_type=jnp.float32,
        )
        odd = lax.broadcasted_iota(jnp.int32, (8, wide), 0) & 1
        total = jnp.zeros((8, wide), jnp.float32)
        for slot in range(27):
            hit = high == odd + 2 * slot
            total = total + jnp.where(hit, found[slot * 8 : slot * 8 + 8], 0.0)
        for c in range(4):
            row = total[2 * c : 2 * c + 1] + total[2 * c + 1 : 2 * c + 2]
            for k in range(4):
                place_ref[c, pl.ds(index * 4 + k, 1), :] = row[:, k * 128 : k * 128 + 128]
        return carry

    lax.fori_loop(0, 32, locate, 0)

    def group(index, carry):
        base = pl.multiple_of(index * rows, rows)
        first = first_ref[pl.ds(base, rows), :]
        second = second_ref[pl.ds(base, rows), :]
        weight = mask_ref[pl.ds(base, rows), :].astype(jnp.float32)
        lane_i = first & 127
        row_i = first >> 7

        def pick(row, lanes):
            wide = jnp.broadcast_to(row, (rows, 128))
            return jnp.take_along_axis(wide, lanes, axis=1, mode="promise_in_bounds")

        zeros = jnp.zeros((rows, 128), jnp.float32)
        place_j = [place_ref[c, pl.ds(base, rows), :] for c in range(4)]
        place_i = [zeros] * 4
        for part in range(4):
            hit = row_i == part
            for c in range(4):
                at = (part & 1) * 8 + c * 2 + (part >> 1)
                place_i[c] = jnp.where(
                    hit, pick(coords_ref[13, at : at + 1, :], lane_i), place_i[c]
                )
        slot = second >> 9
        step_x = (slot * 57) >> 9
        rest = slot - step_x * 9
        step_y = (rest * 11) >> 5
        step_z = rest - step_y * 3
        sep = [
            (place_j[c] + (step.astype(jnp.float32) - 1.0)) - place_i[c]
            for c, step in enumerate((step_x, step_y, step_z))
        ]
        dist_sq = sep[0] * sep[0] + sep[1] * sep[1] + sep[2] * sep[2] + delta_sq
        distance = jnp.sqrt(dist_sq)
        inverse = 1.0 / distance
        exp_minus = jnp.exp(-dist_sq)
        screened = erfc_positive(distance, exp_minus)
        potential = screened * inverse
        slope_coul = -(2.0 / root_pi) * exp_minus * inverse - screened / dist_sq
        envelope = jnp.exp(-0.5 * dist_sq)
        values = (
            sep[0],
            sep[1],
            sep[2],
            distance,
            weight * envelope * inverse,
            weight * coulomb * place_i[3] * place_j[3] * slope_coul * inverse,
            weight * coulomb * place_j[3] * potential,
            weight * coulomb * place_i[3] * potential,
            (first & 255).astype(jnp.float32),
            (first >> 8).astype(jnp.float32),
            (second & 255).astype(jnp.float32),
            (second >> 8).astype(jnp.float32),
        )
        for position, value in enumerate(values):
            out_ref[pl.ds(base, rows), position, :] = value
        return carry

    lax.fori_loop(0, 128 // rows, group, 0)
    out_ref[:, 12:16, :] = jnp.zeros((128, 4, 128), jnp.float32)


def geometry(coords, first, second, mask):
    return pl.pallas_call(
        geometry_kernel,
        out_shape=jax.ShapeDtypeStruct((128, 16, 128), jnp.float32),
        scratch_shapes=[
            pltpu.VMEM((4, 128, 128), jnp.float32),
            pltpu.VMEM((216, 512), jnp.bfloat16),
        ],
        name="geometry",
    )(coords, first, second, mask)


def pair_kernel(
    blocks_ref,
    rows_ref,
    low_ref,
    mid_ref,
    high_ref,
    geo_ref,
    first_ref,
    hidden_ref,
    hidden_t_ref,
    energy_ref,
    back_ref,
    out_low,
    out_mid,
    out_high,
    stage_ref,
    table_ref,
    gather_a,
    gather_b,
    half_a,
    half_b,
    iota_ref,
    term_ref,
    acc_i_ref,
    acc_j_ref,
    sems,
):
    copies = [
        pltpu.make_async_copy(source, stage_ref.at[k], sems.at[k])
        for k, source in enumerate((low_ref, mid_ref, high_ref))
    ]
    for copy in copies:
        copy.start()
    one = jnp.ones((), jnp.bfloat16)
    zero = jnp.zeros((), jnp.bfloat16)
    iota_ref[...] = (
        lax.broadcasted_iota(jnp.int32, (256, 128), 0).astype(jnp.float32).astype(jnp.bfloat16)
    )
    acc_i_ref[...] = jnp.zeros_like(acc_i_ref)
    acc_j_ref[...] = jnp.zeros_like(acc_j_ref)
    term_ref[...] = jnp.zeros_like(term_ref)
    for k in range(3):
        copies[k].wait()

        def widen(step, carry, k=k):
            rows = pl.ds(pl.multiple_of(step * 128, 128), 128)
            table_ref[pl.ds(pl.multiple_of(k * 4608 + step * 128, 128), 128), :] = stage_ref[
                k, rows, :
            ].astype(jnp.float32)
            return carry

        lax.fori_loop(0, 36, widen, 0)

    def fetch(index, gather_ref):
        index = jnp.minimum(index, 63)
        for p in range(chunk):
            row = rows_ref[index * 2 + p // 128, p % 128]
            gather_ref[pl.ds(p, 1), :] = table_ref[pl.ds(row, 1), :]

    def geo_of(index, count):
        return jnp.concatenate([geo_ref[index + k] for k in range(count)], axis=1)

    def equal(rows, row):
        width = row.shape[1]
        iota = jnp.concatenate([iota_ref[0:rows, :]] * (width // 128), axis=1)
        return jnp.where(
            iota == jnp.broadcast_to(row.astype(jnp.bfloat16), (rows, width)), one, zero
        )

    def basis_of(distance):
        offset = distance - (
            0.25 + 0.3 * lax.broadcasted_iota(jnp.int32, (8, chunk), 0).astype(jnp.float32)
        )
        return offset, jnp.exp(-(offset / spread) * (offset / spread))

    def enter(index, gather_ref, half_ref):
        geo = geo_of(jnp.minimum(index, 63) * 2, 2)
        offset, basis = basis_of(geo[3:4])
        top = basis.astype(jnp.bfloat16).astype(jnp.float32)
        low = geo[8:9]
        side = geo[9:10]
        operand = jnp.concatenate(
            [
                equal(256, jnp.where(side == 0.0, low, 512.0)),
                equal(256, jnp.where(side == 0.0, 512.0, low)),
                gather_ref[...].T.astype(jnp.bfloat16),
                jnp.concatenate([top, top, basis - top, jnp.zeros_like(top)], axis=0).astype(
                    jnp.bfloat16
                ),
                jnp.zeros((96, chunk), jnp.bfloat16),
            ],
            axis=0,
        )
        half_ref[...] = jnp.dot(first_ref[...], operand, preferred_element_type=jnp.float32)

    def leave(index, part, half_ref):
        lanes = slice(part * chunk, part * chunk + chunk)
        geo = geo_of(index * 2, 2)
        half_one = half_ref[...]
        bend_one = jnp.tanh(half_one)
        gain_one = 1.0 + bend_one
        act_one = half_one * gain_one
        slope_one = gain_one + act_one * (1.0 - bend_one)
        half_two = jnp.dot(
            hidden_t_ref[...], act_one.astype(jnp.bfloat16), preferred_element_type=jnp.float32
        )
        bend_two = jnp.tanh(half_two)
        gain_two = 1.0 + bend_two
        act_two = half_two * gain_two
        slope_two = gain_two + act_two * (1.0 - bend_two)
        energy = jnp.concatenate([energy_ref[...]] * (chunk // 128), axis=1)
        readout = jnp.sum(act_two * energy, axis=0, keepdims=True)
        back_two = (slope_two * energy).astype(jnp.bfloat16)
        back_one = (
            jnp.dot(hidden_ref[...], back_two, preferred_element_type=jnp.float32) * slope_one
        )
        back_basis = jnp.dot(
            back_ref[...], back_one.astype(jnp.bfloat16), preferred_element_type=jnp.float32
        )
        distance = geo[3:4]
        offset, basis = basis_of(distance)
        total = jnp.sum(
            (back_basis[0:8] + back_basis[8:16])
            * (basis * offset * (-2.0 / (spread * spread))),
            axis=0,
            keepdims=True,
        ) - (readout * distance)
        push = geo[4:5] * total + geo[5:6]
        term_ref[0:3, lanes] = geo[0:3] * push
        term_ref[3:5, lanes] = geo[6:8]

    def deposit(index):
        width = 2 * chunk
        geo = geo_of(jnp.maximum(index, 0) * 4, 4)
        terms = term_ref[...]
        own = terms[0:4]
        own_top = own.astype(jnp.bfloat16).astype(jnp.float32)
        own_rest = own - own_top
        side = geo[9:10]
        own_rows = jnp.concatenate(
            [
                jnp.where(side == half, part, 0.0)
                for half in (0.0, 1.0)
                for part in (own_top, own_rest)
            ],
            axis=0,
        ).astype(jnp.bfloat16)
        acc_i_ref[...] += lax.dot_general(
            own_rows,
            equal(256, geo[8:9]),
            (((1,), (1,)), ((), ())),
            preferred_element_type=jnp.float32,
        )
        far = jnp.concatenate([-terms[0:3], terms[4:5]], axis=0).astype(jnp.bfloat16)
        hit = equal(64, geo[11:12])
        far_rows = jnp.concatenate(
            [hit * jnp.broadcast_to(far[c : c + 1], (64, width)) for c in range(4)], axis=0
        )
        acc_j_ref[...] += lax.dot_general(
            far_rows,
            equal(256, geo[10:11]),
            (((1,), (1,)), ((), ())),
            preferred_element_type=jnp.float32,
        )

    fetch(0, gather_a)
    enter(0, gather_a, half_a)
    fetch(1, gather_b)

    def block(index, carry):
        first = index * 2
        deposit(index - 1)
        enter(first + 1, gather_b, half_b)
        leave(first, 0, half_a)
        fetch(first + 2, gather_a)
        enter(first + 2, gather_a, half_a)
        leave(first + 1, 1, half_b)
        fetch(first + 3, gather_b)
        return carry

    blocks = blocks_ref[0]
    lax.fori_loop(0, blocks, block, 0)
    deposit(blocks - 1)
    acc_i = acc_i_ref[...]
    acc_i = jnp.concatenate([acc_i[0:4] + acc_i[4:8], acc_i[8:12] + acc_i[12:16]], axis=0)
    for c in range(4):
        plane = acc_j_ref[c * 64 : c * 64 + 64, :]
        for slot in range(27):
            step_x, step_y, step_z = slot // 9, slot // 3 % 3, slot % 3
            target = (out_low, out_mid, out_high)[step_y]
            for half in range(2):
                row = plane[slot * 2 + half : slot * 2 + half + 1]
                if slot == 13:
                    row = row + acc_i[half * 4 + c : half * 4 + c + 1]
                target[step_z * 3 + step_x, c * 2 + half : c * 2 + half + 1, :] = row


def pair_sums(block_count, rows, low, mid, high, geo, weights):
    vmem = pl.BlockSpec(memory_space=pltpu.VMEM)
    smem = pl.BlockSpec(memory_space=pltpu.SMEM)
    far = pl.BlockSpec(memory_space=pl.ANY)
    out = jax.ShapeDtypeStruct((9, 8, 256), jnp.float32)
    return pl.pallas_call(
        pair_kernel,
        out_shape=(out, out, out),
        in_specs=[smem, smem, far, far, far, vmem] + [vmem] * 5,
        out_specs=(vmem, vmem, vmem),
        scratch_shapes=[
            pltpu.VMEM((3, 4608, 128), jnp.bfloat16),
            pltpu.VMEM((13824, 128), jnp.float32),
            pltpu.VMEM((chunk, 128), jnp.float32),
            pltpu.VMEM((chunk, 128), jnp.float32),
            pltpu.VMEM((256, chunk), jnp.float32),
            pltpu.VMEM((256, chunk), jnp.float32),
            pltpu.VMEM((256, 128), jnp.bfloat16),
            pltpu.VMEM((8, 2 * chunk), jnp.float32),
            pltpu.VMEM((16, 256), jnp.float32),
            pltpu.VMEM((256, 256), jnp.float32),
            pltpu.SemaphoreType.DMA((3,)),
        ],
        compiler_params=pltpu.CompilerParams(vmem_limit_bytes=48 * 1024 * 1024),
        name="pairs",
    )(block_count, rows, low, mid, high, geo, *weights)


def swap(block, axis):
    count = lax.axis_size(axis)
    forward = [(i, (i + 1) % count) for i in range(count)]
    backward = [(target, source) for source, target in forward]
    return lax.ppermute(block, axis, forward), lax.ppermute(block, axis, backward)


def split(value):
    top = lax.reduce_precision(value, 8, 7)
    return top, value - top


def indices(second_tab, mask_tab, atom_slots):
    slot = second_tab >> 9
    step_x = slot // 9
    step_y = slot // 3 % 3
    step_z = slot % 3
    rows = (step_y * 9 + step_z * 3 + step_x) * atom_slots + (second_tab & (atom_slots - 1))
    busy_tiles = jnp.sum(jnp.any(mask_tab != 0, axis=1).astype(jnp.int32))
    tiles = macro // 128
    block_count = ((busy_tiles + tiles - 1) // tiles).reshape(1)
    return block_count, rows


def arrange(own_feat, w_centre, w_neighbour, w_radial, w_hidden, w_energy):
    centre_t = jnp.dot(own_feat, w_centre, preferred_element_type=jnp.float32).astype(
        jnp.bfloat16
    ).T * jnp.bfloat16(0.5)
    half = jnp.bfloat16(0.5)
    radial_top, radial_rest = split(w_radial * 0.5)
    zero_rows = jnp.zeros_like(radial_top)
    radial_t = (
        jnp.concatenate([radial_top, radial_rest, radial_top, zero_rows], axis=0)
        .astype(jnp.bfloat16)
        .T
    )
    back = jnp.concatenate([radial_top, radial_rest], axis=0).astype(jnp.bfloat16)
    energy = jnp.broadcast_to(w_energy[:, None], (w_energy.shape[0], 128))
    first = jnp.concatenate(
        [centre_t, w_neighbour.T * half, radial_t, jnp.zeros((radial_t.shape[0], 96), jnp.bfloat16)],
        axis=1,
    )
    return (
        first,
        w_hidden * half,
        w_hidden.T * half,
        energy,
        back,
    )


def local(
    features,
    positions,
    counts,
    pair_first,
    pair_second,
    pair_mask,
    w_centre,
    w_neighbour,
    w_charge,
    w_radial,
    w_hidden,
    w_energy,
):
    own_feat = features[0, 0, 0]
    atom_slots = own_feat.shape[0]
    raw_charge = jnp.dot(own_feat, w_charge, preferred_element_type=jnp.float32)
    filled = counts[0, 0, 0]
    alive_slot = jnp.arange(atom_slots, dtype=jnp.int32) < filled
    average = jnp.sum(jnp.where(alive_slot, raw_charge, 0.0)) / filled.astype(jnp.float32)
    charges = jnp.where(alive_slot, raw_charge - average, 0.0)
    coords_own = jnp.concatenate([positions[0, 0, 0], charges[None, :]], axis=0)
    coords_own = coords_own.reshape(8, 2, 128).transpose(1, 0, 2).reshape(16, 128)

    def collect(block):
        low, high = swap(block, "gx")
        line = jnp.stack([low, block, high], axis=0)
        low, high = swap(line, "gz")
        plane = jnp.concatenate([low, line, high], axis=0)
        low, high = swap(plane, "gy")
        return low, plane, high

    near_coords = jnp.stack(collect(coords_own), axis=0)
    low, mid, high = [part.reshape(9 * atom_slots, -1) for part in collect(own_feat)]
    coords_all = (
        near_coords.reshape(3, 3, 3, 16, 128).transpose(2, 0, 1, 3, 4).reshape(27, 16, 128)
    )
    first_tab = pair_first[0, 0, 0]
    second_tab = pair_second[0, 0, 0]
    mask_tab = pair_mask[0, 0, 0]
    geo = geometry(coords_all, first_tab, second_tab, mask_tab)

    block_count, rows = indices(second_tab, mask_tab, atom_slots)
    weights = arrange(own_feat, w_centre, w_neighbour, w_radial, w_hidden, w_energy)
    out_low, out_mid, out_high = pair_sums(block_count, rows, low, mid, high, geo, weights)

    def give(low, mid, high, axis):
        count = lax.axis_size(axis)
        forward = [(i, (i + 1) % count) for i in range(count)]
        backward = [(target, source) for source, target in forward]
        return mid + lax.ppermute(high, axis, forward) + lax.ppermute(low, axis, backward)

    plane = give(out_low, out_mid, out_high, "gy")
    line = give(plane[0:3], plane[3:6], plane[6:9], "gz")
    summed = give(line[0], line[1], line[2], "gx").reshape(4, atom_slots)
    return (summed[:3][None, None, None], summed[3][None, None, None])


def solution(mesh):
    placed = (
        P("gx", "gy", "gz", None, None),
        P("gx", "gy", "gz", None, None),
        P("gx", "gy", "gz"),
        P("gx", "gy", "gz", None, None),
        P("gx", "gy", "gz", None, None),
        P("gx", "gy", "gz", None, None),
        P(),
        P(),
        P(),
        P(),
        P(),
        P(),
    )
    return jax.shard_map(
        local,
        mesh=mesh,
        in_specs=placed,
        out_specs=(P("gx", "gy", "gz", None, None), P("gx", "gy", "gz", None)),
        check_vma=False,
    )
```

```python
import jax
import jax.numpy as jnp
from jax import lax
from jax.experimental import pallas as pl
from jax.experimental.pallas import tpu as pltpu
from jax.sharding import PartitionSpec as P

delta_sq = 0.04
spread = 0.3
coulomb = 0.2
root_pi = 1.7724538509055159
chunk = 512
tiles = chunk // 128
atoms = 512
message = 544
half_message = message // 2
own_pieces = tuple((0, atoms, e * atoms) for e in range(5)) + (
    (0, half_message, 5 * atoms),
    (0, atoms - half_message, 5 * atoms + half_message),
    (0, 3 * atoms, 6 * atoms),
)
side_pieces = ((0, 3 * atoms, 0), (0, 3 * atoms, 3 * atoms), (0, 3 * atoms, 6 * atoms))
pieces = (
    side_pieces
    + tuple((begin, size, 9 * atoms + at) for begin, size, at in own_pieces)
    + tuple((begin, size, 18 * atoms + at) for begin, size, at in side_pieces)
)
piece_count = len(pieces)

erfc_p = (
    2.326819970068386e-2, -1.387039388740657e-1, 3.687424674597105e-1, -5.824733027278666e-1,
    6.210004621745983e-1, -4.944515323274145e-1, 3.404879937665872e-1, -2.741127028184656e-1,
    5.638259427386472e-1,
)
erfc_r = (
    -1.047766399936249e1, 1.297719955372516e1, -7.495518717768503e0, 2.921019019210786e0,
    -1.015265279202700e0, 4.218463358204948e-1, -2.820767439740514e-1, 5.641895067754075e-1,
)
erf_t = (
    7.853861353153693e-5, -8.010193625184903e-4, 5.188327685732524e-3, -2.685381193529856e-2,
    1.128358514861418e-1, -3.761262582423300e-1, 1.128379165726710e0,
)


def poly(x, coefficients):
    total = jnp.full_like(x, coefficients[0])
    for value in coefficients[1:]:
        total = total * x + value
    return total


def erfc_positive(x, exp_minus_sq):
    square = x * x
    inverse = 1.0 / square
    tail = exp_minus_sq / x * jnp.where(x < 2.0, poly(inverse, erfc_p), poly(inverse, erfc_r))
    return jnp.where(x < 1.0, 1.0 - x * poly(square, erf_t), tail)


def geometry_kernel(
    low_ref, mid_ref, high_ref, own_ref, rows_ref, first_ref, second_ref, mask_ref, out_ref,
    place_ref, top_ref,
):
    rows = 32
    wide = 512
    for side, ref in enumerate((low_ref, mid_ref, high_ref)):
        parts = ref[...].astype(jnp.float32)
        for part in range(2):
            at = part * 16
            block = jnp.concatenate([parts[:, at : at + 8], parts[:, at + 8 : at + 16]], axis=2)
            top_ref[side * 72 : side * 72 + 72, part * 256 : part * 256 + 256] = block.reshape(
                72, 256
            ).astype(jnp.bfloat16)

    def locate(index, carry):
        second = jnp.concatenate(
            [rows_ref[pl.ds(index * 4 + k, 1), :] for k in range(4)], axis=1
        )
        low = (second & 255).astype(jnp.float32).astype(jnp.bfloat16)
        high = jnp.broadcast_to(second >> 8, (8, wide))
        iota = lax.broadcasted_iota(jnp.int32, (256, wide), 0).astype(jnp.float32)
        hot = jnp.where(
            iota.astype(jnp.bfloat16) == jnp.broadcast_to(low, (256, wide)),
            jnp.ones((), jnp.bfloat16),
            jnp.zeros((), jnp.bfloat16),
        )
        found = jnp.dot(
            top_ref[...],
            jnp.concatenate([hot, hot], axis=0),
            preferred_element_type=jnp.float32,
        )
        odd = lax.broadcasted_iota(jnp.int32, (8, wide), 0) & 1
        total = jnp.zeros((8, wide), jnp.float32)
        for slot in range(27):
            hit = high == odd + 2 * slot
            total = total + jnp.where(hit, found[slot * 8 : slot * 8 + 8], 0.0)
        for c in range(4):
            row = total[2 * c : 2 * c + 1] + total[2 * c + 1 : 2 * c + 2]
            for k in range(4):
                place_ref[c, pl.ds(index * 4 + k, 1), :] = row[:, k * 128 : k * 128 + 128]
        return carry

    lax.fori_loop(0, 32, locate, 0)

    def group(index, carry):
        base = pl.multiple_of(index * rows, rows)
        first = first_ref[pl.ds(base, rows), :]
        second = second_ref[pl.ds(base, rows), :]
        weight = mask_ref[pl.ds(base, rows), :].astype(jnp.float32)
        lane_i = first & 127
        row_i = first >> 7

        def pick(row, lanes):
            wide = jnp.broadcast_to(row, (rows, 128))
            return jnp.take_along_axis(wide, lanes, axis=1, mode="promise_in_bounds")

        zeros = jnp.zeros((rows, 128), jnp.float32)
        place_j = [place_ref[c, pl.ds(base, rows), :] for c in range(4)]
        place_i = [zeros] * 4
        for part in range(4):
            hit = row_i == part
            for c in range(4):
                at = (part & 1) * 8 + c * 2 + (part >> 1)
                place_i[c] = jnp.where(
                    hit, pick(own_ref[at : at + 1, :], lane_i), place_i[c]
                )
        slot = second >> 9
        step_x = (slot * 57) >> 9
        rest = slot - step_x * 9
        step_y = (rest * 11) >> 5
        step_z = rest - step_y * 3
        sep = [
            (place_j[c] + (step.astype(jnp.float32) - 1.0)) - place_i[c]
            for c, step in enumerate((step_x, step_y, step_z))
        ]
        dist_sq = sep[0] * sep[0] + sep[1] * sep[1] + sep[2] * sep[2] + delta_sq
        distance = jnp.sqrt(dist_sq)
        inverse = 1.0 / distance
        exp_minus = jnp.exp(-dist_sq)
        screened = erfc_positive(distance, exp_minus)
        potential = screened * inverse
        slope_coul = -(2.0 / root_pi) * exp_minus * inverse - screened / dist_sq
        envelope = jnp.exp(-0.5 * dist_sq)
        values = (
            sep[0],
            sep[1],
            sep[2],
            distance,
            weight * envelope * inverse,
            weight * coulomb * place_i[3] * place_j[3] * slope_coul * inverse,
            weight * coulomb * place_j[3] * potential,
            weight * coulomb * place_i[3] * potential,
            (first & 255).astype(jnp.float32),
            (first >> 8).astype(jnp.float32),
            (second & 255).astype(jnp.float32),
            (second >> 8).astype(jnp.float32),
        )
        for position, value in enumerate(values):
            out_ref[pl.ds(base, rows), position, :] = value
        return carry

    lax.fori_loop(0, 128 // rows, group, 0)
    out_ref[:, 12:16, :] = jnp.zeros((128, 4, 128), jnp.float32)


def geometry(parts, own, rows, first, second, mask):
    return pl.pallas_call(
        geometry_kernel,
        out_shape=jax.ShapeDtypeStruct((128, 16, 128), jnp.float32),
        scratch_shapes=[
            pltpu.VMEM((4, 128, 128), jnp.float32),
            pltpu.VMEM((216, 512), jnp.bfloat16),
        ],
        name="geometry",
    )(*parts, own, rows, first, second, mask)


def pair_kernel(
    blocks_ref,
    rows_ref,
    *refs,
):
    sources, refs = refs[:piece_count], refs[piece_count:]
    pair_body(blocks_ref, rows_ref, sources, *refs)


def pair_body(
    blocks_ref,
    rows_ref,
    sources,
    geo_ref,
    first_ref,
    hidden_ref,
    hidden_t_ref,
    energy_ref,
    back_ref,
    out_low,
    out_mid,
    out_high,
    stage_ref,
    table_ref,
    picks_ref,
    gather_ref,
    half_ref,
    slope_ref,
    iota_ref,
    term_ref,
    acc_i_ref,
    acc_j_ref,
    sems,
):
    last = rows_ref.shape[0] - 1

    def picks(index):
        return pltpu.make_async_copy(
            rows_ref.at[jnp.minimum(index, last)], picks_ref, sems.at[piece_count]
        )

    picks(0).start()
    copies = []
    for piece, (source, (begin, size, at)) in enumerate(zip(sources, pieces)):
        copies.append(
            pltpu.make_async_copy(
                source.at[pl.ds(begin, size)], stage_ref.at[pl.ds(at, size)], sems.at[piece]
            )
        )
    for copy in copies:
        copy.start()
    one = jnp.ones((), jnp.bfloat16)
    zero = jnp.zeros((), jnp.bfloat16)
    iota_ref[...] = (
        lax.broadcasted_iota(jnp.int32, (256, 128), 0).astype(jnp.float32).astype(jnp.bfloat16)
    )
    acc_i_ref[...] = jnp.zeros_like(acc_i_ref)
    acc_j_ref[...] = jnp.zeros_like(acc_j_ref)
    term_ref[...] = jnp.zeros_like(term_ref)
    for copy in copies:
        copy.wait()

    def widen(step, carry):
        rows = pl.ds(pl.multiple_of(step * 256, 256), 256)
        table_ref[rows, :] = stage_ref[rows, :].astype(jnp.float32)
        return carry

    lax.fori_loop(0, 54, widen, 0)

    def fetch():
        for p in range(chunk):
            row = picks_ref[p // 128, p % 128]
            gather_ref[pl.ds(p, 1), :] = table_ref[pl.ds(row, 1), :]

    def geo_of(index):
        return jnp.concatenate([geo_ref[index * tiles + k] for k in range(tiles)], axis=1)

    def equal(rows, row):
        width = row.shape[1]
        iota = jnp.concatenate([iota_ref[0:rows, :]] * (width // 128), axis=1)
        return jnp.where(
            iota == jnp.broadcast_to(row.astype(jnp.bfloat16), (rows, width)), one, zero
        )

    def basis_of(distance):
        offset = distance - (
            0.25 + 0.3 * lax.broadcasted_iota(jnp.int32, (8, chunk), 0).astype(jnp.float32)
        )
        return offset, jnp.exp(-(offset / spread) * (offset / spread))

    def enter(index):
        geo = geo_of(jnp.minimum(index, last))
        offset, basis = basis_of(geo[3:4])
        top = basis.astype(jnp.bfloat16).astype(jnp.float32)
        low = geo[8:9]
        side = geo[9:10]
        operand = jnp.concatenate(
            [
                equal(256, jnp.where(side == 0.0, low, 512.0)),
                equal(256, jnp.where(side == 0.0, 512.0, low)),
                gather_ref[...].T.astype(jnp.bfloat16),
                jnp.concatenate([top, top, basis - top, jnp.zeros_like(top)], axis=0).astype(
                    jnp.bfloat16
                ),
                jnp.zeros((96, chunk), jnp.bfloat16),
            ],
            axis=0,
        )
        half_ref[...] = jnp.dot(first_ref[...], operand, preferred_element_type=jnp.float32)

    def activate():
        half_one = half_ref[...]
        bend_one = jnp.tanh(half_one)
        gain_one = 1.0 + bend_one
        act_one = half_one * gain_one
        slope_ref[...] = gain_one + act_one * (1.0 - bend_one)
        return act_one.astype(jnp.bfloat16)

    def finish(index, act_one):
        geo = geo_of(index)
        half_two = jnp.dot(hidden_t_ref[...], act_one, preferred_element_type=jnp.float32)
        bend_two = jnp.tanh(half_two)
        gain_two = 1.0 + bend_two
        act_two = half_two * gain_two
        slope_two = gain_two + act_two * (1.0 - bend_two)
        energy = jnp.concatenate([energy_ref[...]] * tiles, axis=1)
        readout = jnp.sum(act_two * energy, axis=0, keepdims=True)
        back_two = (slope_two * energy).astype(jnp.bfloat16)
        back_one = jnp.dot(hidden_ref[...], back_two, preferred_element_type=jnp.float32)
        back_one = (back_one * slope_ref[...]).astype(jnp.bfloat16)
        back_basis = jnp.dot(back_ref[...], back_one, preferred_element_type=jnp.float32)
        distance = geo[3:4]
        offset, basis = basis_of(distance)
        total = jnp.sum(
            (back_basis[0:8] + back_basis[8:16])
            * (basis * offset * (-2.0 / (spread * spread))),
            axis=0,
            keepdims=True,
        ) - (readout * distance)
        push = geo[4:5] * total + geo[5:6]
        term_ref[0:3, :] = geo[0:3] * push
        term_ref[3:5, :] = geo[6:8]

    def deposit(index):
        geo = geo_of(jnp.maximum(index, 0))
        terms = term_ref[...]
        own = terms[0:4]
        own_top = own.astype(jnp.bfloat16).astype(jnp.float32)
        own_rest = own - own_top
        side = geo[9:10]
        own_rows = jnp.concatenate(
            [
                jnp.where(side == half, part, 0.0)
                for half in (0.0, 1.0)
                for part in (own_top, own_rest)
            ],
            axis=0,
        ).astype(jnp.bfloat16)
        acc_i_ref[...] += lax.dot_general(
            own_rows,
            equal(256, geo[8:9]),
            (((1,), (1,)), ((), ())),
            preferred_element_type=jnp.float32,
        )
        far = jnp.concatenate([-terms[0:3], terms[4:5]], axis=0).astype(jnp.bfloat16)
        hit = equal(64, geo[11:12])
        far_rows = jnp.concatenate(
            [hit * jnp.broadcast_to(far[c : c + 1], (64, chunk)) for c in range(4)], axis=0
        )
        acc_j_ref[...] += lax.dot_general(
            far_rows,
            equal(256, geo[10:11]),
            (((1,), (1,)), ((), ())),
            preferred_element_type=jnp.float32,
        )

    picks(0).wait()
    fetch()
    picks(1).start()
    enter(0)
    picks(1).wait()
    fetch()
    picks(2).start()

    def block(index, carry):
        picks(index + 2).wait()
        act_one = activate()
        deposit(index - 1)
        enter(index + 1)
        fetch()
        finish(index, act_one)
        picks(index + 3).start()
        return carry

    blocks = blocks_ref[0]
    lax.fori_loop(0, blocks, block, 0)
    picks(blocks + 2).wait()
    deposit(blocks - 1)
    acc_i = acc_i_ref[...]
    acc_i = jnp.concatenate([acc_i[0:4] + acc_i[4:8], acc_i[8:12] + acc_i[12:16]], axis=0)
    for c in range(4):
        plane = acc_j_ref[c * 64 : c * 64 + 64, :]
        for slot in range(27):
            step_x, step_y, step_z = slot // 9, slot // 3 % 3, slot % 3
            target = (out_low, out_mid, out_high)[step_y]
            for half in range(2):
                row = plane[slot * 2 + half : slot * 2 + half + 1]
                if slot == 13:
                    row = row + acc_i[half * 4 + c : half * 4 + c + 1]
                target[step_z * 3 + step_x, c * 2 + half : c * 2 + half + 1, :] = row


def pair_sums(block_count, rows, features, geo, weights):
    vmem = pl.BlockSpec(memory_space=pltpu.VMEM)
    smem = pl.BlockSpec(memory_space=pltpu.SMEM)
    far = pl.BlockSpec(memory_space=pl.ANY)
    out = jax.ShapeDtypeStruct((9, 8, 256), jnp.float32)
    return pl.pallas_call(
        pair_kernel,
        out_shape=(out, out, out),
        in_specs=[smem, far] + [far] * piece_count + [vmem] * 6,
        out_specs=(vmem, vmem, vmem),
        scratch_shapes=[
            pltpu.VMEM((13824, 128), jnp.bfloat16),
            pltpu.VMEM((13824, 128), jnp.float32),
            pltpu.SMEM((tiles, 128), jnp.int32),
            pltpu.VMEM((chunk, 128), jnp.float32),
            pltpu.VMEM((256, chunk), jnp.float32),
            pltpu.VMEM((256, chunk), jnp.float32),
            pltpu.VMEM((256, 128), jnp.bfloat16),
            pltpu.VMEM((8, chunk), jnp.float32),
            pltpu.VMEM((16, 256), jnp.float32),
            pltpu.VMEM((256, 256), jnp.float32),
            pltpu.SemaphoreType.DMA((piece_count + 1,)),
        ],
        compiler_params=pltpu.CompilerParams(vmem_limit_bytes=48 * 1024 * 1024),
        name="pairs",
    )(block_count, rows, *features, geo, *weights)


def swap(block, axis):
    count = lax.axis_size(axis)
    forward = [(i, (i + 1) % count) for i in range(count)]
    backward = [(target, source) for source, target in forward]
    return lax.ppermute(block, axis, forward), lax.ppermute(block, axis, backward)


def lines():
    length = lax.axis_size("gz")
    up = []
    for x in range(lax.axis_size("gx")):
        for z in range(length):
            target = (x, z + 1) if z + 1 < length else (x ^ 1, 0)
            up.append((x * length + z, target[0] * length + target[1]))
    return up, [(target, source) for source, target in up]


def carry_across(block):
    count = lax.axis_size("gx")
    return lax.ppermute(
        block, "gx", [(i, (i + 2) % count if i % 2 == 0 else (i - 2) % count) for i in range(count)]
    )


def collect(brick):
    up, down = lines()
    line = ("gx", "gz")
    u1 = lax.ppermute(brick, line, up)
    d1 = lax.ppermute(brick, line, down)
    early = jnp.concatenate([brick[:atoms], u1[:atoms], d1[:atoms]], axis=0)
    early_low, early_high = swap(early, "gy")
    u2 = lax.ppermute(u1, line, up)
    d2 = lax.ppermute(d1, line, down)
    u3 = lax.ppermute(u2, line, up)
    d3 = lax.ppermute(d2, line, down)
    u4 = lax.ppermute(u3[:half_message], line, up)
    d4 = lax.ppermute(d3[half_message:], line, down)
    place = lax.axis_index("gz")
    low = jnp.where(place == 0, u1, d3)
    high = jnp.where(place == lax.axis_size("gz") - 1, d1, u3)
    tail = atoms - half_message
    far_coords = carry_across(
        jnp.concatenate([low[atoms:], d4[tail:], high[atoms:]], axis=0)
    )
    far = carry_across(jnp.concatenate([low[:atoms], u4, d4[:tail], high[:atoms]], axis=0))
    coords = jnp.concatenate(
        [part[atoms:] for part in (brick, u1, d1, u3, d3)] + [d4[tail:], far_coords], axis=0
    )
    coords_low, coords_high = swap(coords, "gy")
    late = jnp.concatenate([u3[:atoms], d3[:atoms], u4, d4[:tail]], axis=0)
    late_low, late_high = swap(late, "gy")
    far_low, far_high = swap(far, "gy")
    features = (
        (early_low, late_low, far_low)
        + (brick, u1, d1, u3, d3, u4, d4, far)
        + (early_high, late_high, far_high)
    )
    coords = [part.reshape(9, 32, 128) for part in (coords_low, coords, coords_high)]
    return features, coords


def block_of(slot):
    step_x = slot // 9 - 1
    step_y = slot // 3 % 3
    step_z = slot % 3 - 1
    place = lax.axis_index("gz")
    bottom = place == 0
    top = place == lax.axis_size("gz") - 1
    partner = 1 - 2 * (lax.axis_index("gx") % 2)
    same = jnp.where(
        step_z == 0, 0, jnp.where(step_z < 0, jnp.where(bottom, 4, 1), jnp.where(top, 3, 2))
    )
    beside = jnp.where(
        step_z == 0, 5, jnp.where(step_z < 0, jnp.where(bottom, 1, 4), jnp.where(top, 2, 3))
    )
    column = jnp.where(
        step_x == 0, same, jnp.where(step_x == partner, beside, 7 + step_z)
    )
    return step_y * 9 + column


def split(value):
    top = lax.reduce_precision(value, 8, 7)
    return top, value - top


def busy_blocks(mask_tab):
    busy_tiles = jnp.sum(jnp.any(mask_tab != 0, axis=1).astype(jnp.int32))
    return ((busy_tiles + tiles - 1) // tiles).reshape(1)


def arrange(own_feat, w_centre, w_neighbour, w_radial, w_hidden, w_energy):
    centre_t = jnp.dot(own_feat, w_centre, preferred_element_type=jnp.float32).astype(
        jnp.bfloat16
    ).T * jnp.bfloat16(0.5)
    half = jnp.bfloat16(0.5)
    radial_top, radial_rest = split(w_radial * 0.5)
    zero_rows = jnp.zeros_like(radial_top)
    radial_t = (
        jnp.concatenate([radial_top, radial_rest, radial_top, zero_rows], axis=0)
        .astype(jnp.bfloat16)
        .T
    )
    back = jnp.concatenate([radial_top, radial_rest], axis=0).astype(jnp.bfloat16)
    energy = jnp.broadcast_to(w_energy[:, None], (w_energy.shape[0], 128))
    first = jnp.concatenate(
        [centre_t, w_neighbour.T * half, radial_t, jnp.zeros((radial_t.shape[0], 96), jnp.bfloat16)],
        axis=1,
    )
    return (
        first,
        w_hidden * half,
        w_hidden.T * half,
        energy,
        back,
    )


def local(
    features,
    positions,
    counts,
    pair_first,
    pair_second,
    pair_mask,
    w_centre,
    w_neighbour,
    w_charge,
    w_radial,
    w_hidden,
    w_energy,
):
    own_feat = features[0, 0, 0]
    atom_slots = own_feat.shape[0]
    raw_charge = jnp.dot(own_feat, w_charge, preferred_element_type=jnp.float32)
    filled = counts[0, 0, 0]
    alive_slot = jnp.arange(atom_slots, dtype=jnp.int32) < filled
    average = jnp.sum(jnp.where(alive_slot, raw_charge, 0.0)) / filled.astype(jnp.float32)
    charges = jnp.where(alive_slot, raw_charge - average, 0.0)
    coords_own = jnp.concatenate([positions[0, 0, 0], charges[None, :]], axis=0)
    coords_own = coords_own.reshape(8, 2, 128).transpose(1, 0, 2).reshape(16, 128)

    coords_top, coords_rest = split(coords_own)
    brick = jnp.concatenate(
        [own_feat, coords_top.astype(jnp.bfloat16), coords_rest.astype(jnp.bfloat16)], axis=0
    )
    features, coords = collect(brick)
    first_tab = pair_first[0, 0, 0]
    second_tab = pair_second[0, 0, 0]
    mask_tab = pair_mask[0, 0, 0]
    rows = block_of(second_tab // atoms) * atoms + second_tab % atoms
    geo = geometry(coords, coords_own, rows, first_tab, second_tab, mask_tab)
    weights = arrange(own_feat, w_centre, w_neighbour, w_radial, w_hidden, w_energy)
    out_low, out_mid, out_high = pair_sums(
        busy_blocks(mask_tab), rows.reshape(-1, tiles, 128), features, geo, weights
    )

    def give(low, mid, high, axis):
        count = lax.axis_size(axis)
        forward = [(i, (i + 1) % count) for i in range(count)]
        backward = [(target, source) for source, target in forward]
        return mid + lax.ppermute(high, axis, forward) + lax.ppermute(low, axis, backward)

    plane = give(out_low, out_mid, out_high, "gy")
    line = give(plane[0:3], plane[3:6], plane[6:9], "gz")
    summed = give(line[0], line[1], line[2], "gx").reshape(4, atom_slots)
    return (summed[:3][None, None, None], summed[3][None, None, None])


def solution(mesh):
    placed = (
        P("gx", "gy", "gz", None, None),
        P("gx", "gy", "gz", None, None),
        P("gx", "gy", "gz"),
        P("gx", "gy", "gz", None, None),
        P("gx", "gy", "gz", None, None),
        P("gx", "gy", "gz", None, None),
        P(),
        P(),
        P(),
        P(),
        P(),
        P(),
    )
    return jax.shard_map(
        local,
        mesh=mesh,
        in_specs=placed,
        out_specs=(P("gx", "gy", "gz", None, None), P("gx", "gy", "gz", None)),
        check_vma=False,
    )
```

```python
import jax
import jax.numpy as jnp
from jax import lax
from jax.experimental import pallas as pl
from jax.experimental.pallas import tpu as pltpu
from jax.sharding import PartitionSpec as P

delta_sq = 0.04
spread = 0.3
coulomb = 0.2
root_pi = 1.7724538509055159
chunk = 512
tiles = chunk // 128
atoms = 512
message = 544
half_message = message // 2
group = 3 * message
side_bricks = tuple((piece, e * message) for piece in range(3) for e in range(3))
own_bricks = tuple((piece, 0) for piece in range(5)) + (None,) + tuple(
    (7, e * message) for e in range(3)
)


def copy_list():
    features, coords = [], []
    for side, (base, bricks) in enumerate(((0, side_bricks), (3, own_bricks), (11, side_bricks))):
        for e, brick in enumerate(bricks):
            block = side * 9 + e
            at = block * atoms
            if brick is None:
                rest = atoms - half_message
                features.append((base + 5, 0, half_message, at))
                features.append((base + 6, 0, rest, at + half_message))
                coords.append((base + 6, rest, block))
            else:
                piece, begin = brick
                features.append((base + piece, begin, atoms, at))
                coords.append((base + piece, begin + atoms, block))
    return features, coords


piece_count = 14
weight_count = 5
feature_copies, coord_copies = copy_list()
copy_count = len(feature_copies) + len(coord_copies) + weight_count + 1

erfc_p = (
    2.326819970068386e-2, -1.387039388740657e-1, 3.687424674597105e-1, -5.824733027278666e-1,
    6.210004621745983e-1, -4.944515323274145e-1, 3.404879937665872e-1, -2.741127028184656e-1,
    5.638259427386472e-1,
)
erfc_r = (
    -1.047766399936249e1, 1.297719955372516e1, -7.495518717768503e0, 2.921019019210786e0,
    -1.015265279202700e0, 4.218463358204948e-1, -2.820767439740514e-1, 5.641895067754075e-1,
)
erf_t = (
    7.853861353153693e-5, -8.010193625184903e-4, 5.188327685732524e-3, -2.685381193529856e-2,
    1.128358514861418e-1, -3.761262582423300e-1, 1.128379165726710e0,
)


def poly(x, coefficients):
    total = jnp.full_like(x, coefficients[0])
    for value in coefficients[1:]:
        total = total * x + value
    return total


def erfc_positive(x, exp_minus_sq):
    square = x * x
    inverse = 1.0 / square
    tail = exp_minus_sq / x * jnp.where(x < 2.0, poly(inverse, erfc_p), poly(inverse, erfc_r))
    return jnp.where(x < 1.0, 1.0 - x * poly(square, erf_t), tail)


def geometry_phase(
    coords_ref, rows_ref, first_ref, second_ref, mask_ref, out_ref, place_ref, top_ref, iota_ref
):
    rows = 32
    wide = 512
    own = coords_ref[9, 0:16, :].astype(jnp.float32) + coords_ref[9, 16:32, :].astype(
        jnp.float32
    )
    for side in range(3):
        parts = coords_ref[side * 9 : side * 9 + 9].astype(jnp.float32)
        for part in range(2):
            at = part * 16
            block = jnp.concatenate([parts[:, at : at + 8], parts[:, at + 8 : at + 16]], axis=2)
            top_ref[side * 72 : side * 72 + 72, part * 256 : part * 256 + 256] = block.reshape(
                72, 256
            ).astype(jnp.bfloat16)

    def locate(index, carry):
        second = jnp.concatenate(
            [rows_ref[index, k : k + 1, :] for k in range(4)], axis=1
        )
        low = (second & 255).astype(jnp.float32).astype(jnp.bfloat16)
        high = jnp.broadcast_to(second >> 8, (8, wide))
        hot = jnp.where(
            jnp.concatenate([iota_ref[...]] * 4, axis=1) == jnp.broadcast_to(low, (256, wide)),
            jnp.ones((), jnp.bfloat16),
            jnp.zeros((), jnp.bfloat16),
        )
        found = jnp.dot(
            top_ref[...],
            jnp.concatenate([hot, hot], axis=0),
            preferred_element_type=jnp.float32,
        )
        odd = lax.broadcasted_iota(jnp.int32, (8, wide), 0) & 1
        total = jnp.zeros((8, wide), jnp.float32)
        for slot in range(27):
            hit = high == odd + 2 * slot
            total = total + jnp.where(hit, found[slot * 8 : slot * 8 + 8], 0.0)
        for c in range(4):
            row = total[2 * c : 2 * c + 1] + total[2 * c + 1 : 2 * c + 2]
            for k in range(4):
                place_ref[c, pl.ds(index * 4 + k, 1), :] = row[:, k * 128 : k * 128 + 128]
        return carry

    lax.fori_loop(0, 32, locate, 0, unroll=2)

    def group(index, carry):
        base = pl.multiple_of(index * rows, rows)
        first = first_ref[pl.ds(base, rows), :]
        second = second_ref[pl.ds(base, rows), :]
        weight = mask_ref[pl.ds(base, rows), :].astype(jnp.float32)
        lane_i = first & 127
        row_i = first >> 7

        def pick(row, lanes):
            wide = jnp.broadcast_to(row, (rows, 128))
            return jnp.take_along_axis(wide, lanes, axis=1, mode="promise_in_bounds")

        zeros = jnp.zeros((rows, 128), jnp.float32)
        place_j = [place_ref[c, pl.ds(base, rows), :] for c in range(4)]
        place_i = [zeros] * 4
        for part in range(4):
            hit = row_i == part
            for c in range(4):
                at = (part & 1) * 8 + c * 2 + (part >> 1)
                place_i[c] = jnp.where(
                    hit, pick(own[at : at + 1], lane_i), place_i[c]
                )
        slot = second >> 9
        step_x = (slot * 57) >> 9
        rest = slot - step_x * 9
        step_y = (rest * 11) >> 5
        step_z = rest - step_y * 3
        sep = [
            (place_j[c] + (step.astype(jnp.float32) - 1.0)) - place_i[c]
            for c, step in enumerate((step_x, step_y, step_z))
        ]
        dist_sq = sep[0] * sep[0] + sep[1] * sep[1] + sep[2] * sep[2] + delta_sq
        distance = jnp.sqrt(dist_sq)
        inverse = 1.0 / distance
        exp_minus = jnp.exp(-dist_sq)
        screened = erfc_positive(distance, exp_minus)
        potential = screened * inverse
        slope_coul = -(2.0 / root_pi) * exp_minus * inverse - screened / dist_sq
        envelope = jnp.exp(-0.5 * dist_sq)
        values = (
            sep[0],
            sep[1],
            sep[2],
            distance,
            weight * envelope * inverse,
            weight * coulomb * place_i[3] * place_j[3] * slope_coul * inverse,
            weight * coulomb * place_j[3] * potential,
            weight * coulomb * place_i[3] * potential,
            (first & 255).astype(jnp.float32),
            (first >> 8).astype(jnp.float32),
            (second & 255).astype(jnp.float32),
            (second >> 8).astype(jnp.float32),
        )
        for position, value in enumerate(values):
            out_ref[pl.ds(base, rows), position, :] = value
        return carry

    lax.fori_loop(0, 128 // rows, group, 0)
    out_ref[:, 12:16, :] = jnp.zeros((128, 4, 128), jnp.float32)


def brick_kernel(features_ref, positions_ref, counts_ref, charge_ref, out_ref):
    features = features_ref[...]
    weight = jnp.broadcast_to(charge_ref[...], (8, 128))
    raw = lax.dot_general(
        weight, features, (((1,), (1,)), ((), ())), preferred_element_type=jnp.float32
    )[0:1]
    filled = counts_ref[0]
    alive = lax.broadcasted_iota(jnp.int32, (1, atoms), 1) < filled
    total = jnp.sum(jnp.where(alive, raw, 0.0), axis=1, keepdims=True)
    charges = jnp.where(alive, raw - total / filled.astype(jnp.float32), 0.0)
    halves = [positions_ref[c : c + 1, 256 * h : 256 * h + 256] for c in range(3) for h in range(2)]
    halves += [charges[:, 0:256], charges[:, 256:512]]
    coords = jnp.concatenate(halves, axis=0)
    coords = jnp.concatenate([coords[:, 0:128], coords[:, 128:256]], axis=0)
    top = coords.astype(jnp.bfloat16)
    out_ref[0:atoms, :] = features
    out_ref[atoms : atoms + 16, :] = top
    out_ref[atoms + 16 : message, :] = (coords - top.astype(jnp.float32)).astype(jnp.bfloat16)


def make_brick(features, positions, counts, w_charge):
    vmem = pl.BlockSpec(memory_space=pltpu.VMEM)
    return pl.pallas_call(
        brick_kernel,
        out_shape=jax.ShapeDtypeStruct((message, 128), jnp.bfloat16),
        in_specs=[vmem, vmem, pl.BlockSpec(memory_space=pltpu.SMEM), vmem],
        name="brick",
    )(features, positions, counts, w_charge)


def arrange_kernel(
    brick_ref, centre_ref, neighbour_ref, radial_ref, hidden_ref, energy_ref,
    first_out, half_out, turned_out, energy_out, back_out,
):
    centre = lax.dot_general(
        centre_ref[...],
        brick_ref[0:atoms, :],
        (((0,), (1,)), ((), ())),
        preferred_element_type=jnp.float32,
    )
    first_out[:, 0:512] = (centre.astype(jnp.bfloat16).astype(jnp.float32) * 0.5).astype(
        jnp.bfloat16
    )
    first_out[:, 512:640] = (neighbour_ref[...].astype(jnp.float32).T * 0.5).astype(jnp.bfloat16)
    radial = radial_ref[...] * 0.5
    top = radial.astype(jnp.bfloat16).astype(jnp.float32)
    rest = radial - top
    side = jnp.concatenate([top, rest, top, jnp.zeros((104, 256), jnp.float32)], axis=0)
    first_out[:, 640:768] = side.T.astype(jnp.bfloat16)
    hidden = hidden_ref[...].astype(jnp.float32) * 0.5
    half_out[...] = hidden.astype(jnp.bfloat16)
    turned_out[...] = hidden.T.astype(jnp.bfloat16)
    energy_out[...] = jnp.broadcast_to(energy_ref[...], (128, 256)).T
    back_out[...] = jnp.concatenate([top, rest], axis=0).astype(jnp.bfloat16)


def arrange(brick, w_centre, w_neighbour, w_radial, w_hidden, w_energy):
    def shape(rows, columns, kind=jnp.bfloat16):
        return jax.ShapeDtypeStruct((rows, columns), kind)

    return pl.pallas_call(
        arrange_kernel,
        out_shape=(
            shape(256, 768),
            shape(256, 256),
            shape(256, 256),
            shape(256, 128, jnp.float32),
            shape(16, 256),
        ),
        name="arrange",
    )(brick, w_centre, w_neighbour, w_radial, w_hidden, w_energy.reshape(1, -1))


def pair_kernel(rows_ref, pick_first, pick_second, pick_mask, *refs):
    pair_body(
        rows_ref,
        pick_first,
        pick_second,
        pick_mask,
        refs[:piece_count],
        refs[piece_count : piece_count + weight_count],
        *refs[piece_count + weight_count :],
    )


def pair_body(
    rows_ref,
    pick_first,
    pick_second,
    pick_mask,
    sources,
    weights,
    out_low,
    out_mid,
    out_high,
    first_ref,
    hidden_ref,
    hidden_t_ref,
    energy_ref,
    back_ref,
    stage_ref,
    coords_ref,
    place_ref,
    top_ref,
    geo_ref,
    table_ref,
    picks_ref,
    gather_ref,
    feature_ref,
    half_ref,
    slope_ref,
    iota_ref,
    term_ref,
    acc_i_ref,
    acc_j_ref,
    sems,
):
    last = rows_ref.shape[0] - 1

    def picks(index):
        return pltpu.make_async_copy(
            rows_ref.at[jnp.minimum(index, last)], picks_ref, sems.at[copy_count - 1]
        )

    picks(0).start()
    plan = [
        (sources[piece].at[pl.ds(begin, 32)], coords_ref.at[block])
        for piece, begin, block in coord_copies
    ]
    plan += [
        (sources[piece].at[pl.ds(begin, size)], stage_ref.at[pl.ds(at, size)])
        for piece, begin, size, at in feature_copies
    ]
    plan += list(zip(weights, (first_ref, hidden_ref, hidden_t_ref, energy_ref, back_ref)))
    copies = [
        pltpu.make_async_copy(source, target, sems.at[k])
        for k, (source, target) in enumerate(plan)
    ]
    for copy in copies:
        copy.start()
    one = jnp.ones((), jnp.bfloat16)
    zero = jnp.zeros((), jnp.bfloat16)
    iota_ref[...] = (
        lax.broadcasted_iota(jnp.int32, (256, 128), 0).astype(jnp.float32).astype(jnp.bfloat16)
    )
    acc_i_ref[...] = jnp.zeros_like(acc_i_ref)
    acc_j_ref[...] = jnp.zeros_like(acc_j_ref)
    term_ref[...] = jnp.zeros_like(term_ref)
    for copy in copies[: len(coord_copies)]:
        copy.wait()
    geometry_phase(
        coords_ref, rows_ref, pick_first, pick_second, pick_mask, geo_ref, place_ref, top_ref,
        iota_ref,
    )
    tile = lax.broadcasted_iota(jnp.int32, (128, 128), 0) + tiles
    blocks = jnp.max(jnp.where(pick_mask[...] != 0, tile, 0)) // tiles
    for copy in copies[len(coord_copies) :]:
        copy.wait()

    def widen(step, carry):
        rows = pl.ds(pl.multiple_of(step * 256, 256), 256)
        table_ref[rows, :] = stage_ref[rows, :].astype(jnp.float32)
        return carry

    lax.fori_loop(0, 54, widen, 0)

    def fetch(*parts):
        for part in parts or range(tiles):
            for p in range(part * 128, part * 128 + 128):
                row = picks_ref[part, p % 128]
                gather_ref[pl.ds(p, 1), :] = table_ref[pl.ds(row, 1), :]

    def turn():
        feature_ref[...] = gather_ref[...].T.astype(jnp.bfloat16)

    def geo_of(index):
        return jnp.concatenate([geo_ref[index * tiles + k] for k in range(tiles)], axis=1)

    def equal(rows, row):
        width = row.shape[1]
        iota = jnp.concatenate([iota_ref[0:rows, :]] * (width // 128), axis=1)
        return jnp.where(
            iota == jnp.broadcast_to(row.astype(jnp.bfloat16), (rows, width)), one, zero
        )

    def basis_of(distance):
        offset = distance - (
            0.25 + 0.3 * lax.broadcasted_iota(jnp.int32, (8, chunk), 0).astype(jnp.float32)
        )
        return offset, jnp.exp(-(offset / spread) * (offset / spread))

    def enter(index):
        geo = geo_of(jnp.minimum(index, last))
        offset, basis = basis_of(geo[3:4])
        top = basis.astype(jnp.bfloat16).astype(jnp.float32)
        low = geo[8:9]
        side = geo[9:10]
        operand = jnp.concatenate(
            [
                equal(256, jnp.where(side == 0.0, low, 512.0)),
                equal(256, jnp.where(side == 0.0, 512.0, low)),
                feature_ref[...],
                jnp.concatenate([top, top, basis - top, jnp.zeros_like(top)], axis=0).astype(
                    jnp.bfloat16
                ),
                jnp.zeros((96, chunk), jnp.bfloat16),
            ],
            axis=0,
        )
        half_ref[...] = jnp.dot(first_ref[...], operand, preferred_element_type=jnp.float32)

    def activate():
        half_one = half_ref[...]
        bend_one = jnp.tanh(half_one)
        gain_one = 1.0 + bend_one
        act_one = half_one * gain_one
        slope_ref[...] = gain_one + act_one * (1.0 - bend_one)
        return act_one.astype(jnp.bfloat16)

    def second(half_two):
        bend_two = jnp.tanh(half_two)
        gain_two = 1.0 + bend_two
        act_two = half_two * gain_two
        slope_two = gain_two + act_two * (1.0 - bend_two)
        energy = jnp.concatenate([energy_ref[...]] * tiles, axis=1)
        readout = jnp.sum(act_two * energy, axis=0, keepdims=True)
        return readout, (slope_two * energy).astype(jnp.bfloat16)

    def finish(index, readout, back_one):
        geo = geo_of(index)
        back_basis = jnp.dot(back_ref[...], back_one, preferred_element_type=jnp.float32)
        distance = geo[3:4]
        offset, basis = basis_of(distance)
        total = jnp.sum(
            (back_basis[0:8] + back_basis[8:16])
            * (basis * offset * (-2.0 / (spread * spread))),
            axis=0,
            keepdims=True,
        ) - (readout * distance)
        push = geo[4:5] * total + geo[5:6]
        term_ref[0:3, :] = geo[0:3] * push
        term_ref[3:5, :] = geo[6:8]

    def deposit(index):
        geo = geo_of(jnp.maximum(index, 0))
        terms = term_ref[...]
        own = terms[0:4]
        own_top = own.astype(jnp.bfloat16).astype(jnp.float32)
        own_rest = own - own_top
        side = geo[9:10]
        own_rows = jnp.concatenate(
            [
                jnp.where(side == half, part, 0.0)
                for half in (0.0, 1.0)
                for part in (own_top, own_rest)
            ],
            axis=0,
        ).astype(jnp.bfloat16)
        acc_i_ref[...] += lax.dot_general(
            own_rows,
            equal(256, geo[8:9]),
            (((1,), (1,)), ((), ())),
            preferred_element_type=jnp.float32,
        )
        far = jnp.concatenate([-terms[0:3], terms[4:5]], axis=0).astype(jnp.bfloat16)
        hit = equal(64, geo[11:12])
        far_rows = jnp.concatenate(
            [hit * jnp.broadcast_to(far[c : c + 1], (64, chunk)) for c in range(4)], axis=0
        )
        acc_j_ref[...] += lax.dot_general(
            far_rows,
            equal(256, geo[10:11]),
            (((1,), (1,)), ((), ())),
            preferred_element_type=jnp.float32,
        )

    picks(0).wait()
    fetch()
    picks(1).start()
    turn()
    enter(0)
    picks(1).wait()
    fetch()
    picks(2).start()

    def block(index, carry):
        picks(index + 2).wait()
        act_one = activate()
        half_two = jnp.dot(hidden_t_ref[...], act_one, preferred_element_type=jnp.float32)
        turn()
        enter(index + 1)
        fetch()
        readout, back_two = second(half_two)
        deposit(index - 1)
        back_one = jnp.dot(hidden_ref[...], back_two, preferred_element_type=jnp.float32)
        back_one = (back_one * slope_ref[...]).astype(jnp.bfloat16)
        finish(index, readout, back_one)
        picks(index + 3).start()
        return carry

    lax.fori_loop(0, blocks, block, 0)
    picks(blocks + 2).wait()
    deposit(blocks - 1)
    acc_i = acc_i_ref[...]
    acc_i = jnp.concatenate([acc_i[0:4] + acc_i[4:8], acc_i[8:12] + acc_i[12:16]], axis=0)
    for c in range(4):
        plane = acc_j_ref[c * 64 : c * 64 + 64, :]
        for slot in range(27):
            step_x, step_y, step_z = slot // 9, slot // 3 % 3, slot % 3
            target = (out_low, out_mid, out_high)[step_y]
            for half in range(2):
                row = plane[slot * 2 + half : slot * 2 + half + 1]
                if slot == 13:
                    row = row + acc_i[half * 4 + c : half * 4 + c + 1]
                target[step_z * 3 + step_x, c * 2 + half : c * 2 + half + 1, :] = row


def pair_sums(rows, first, second, mask, features, weights):
    vmem = pl.BlockSpec(memory_space=pltpu.VMEM)
    far = pl.BlockSpec(memory_space=pltpu.HBM)
    out = jax.ShapeDtypeStruct((9, 8, 256), jnp.float32)
    return pl.pallas_call(
        pair_kernel,
        out_shape=(out, out, out),
        in_specs=[vmem] * 4 + [far] * (piece_count + weight_count),
        out_specs=(vmem, vmem, vmem),
        scratch_shapes=[
            pltpu.VMEM((256, 768), jnp.bfloat16),
            pltpu.VMEM((256, 256), jnp.bfloat16),
            pltpu.VMEM((256, 256), jnp.bfloat16),
            pltpu.VMEM((256, 128), jnp.float32),
            pltpu.VMEM((16, 256), jnp.bfloat16),
            pltpu.VMEM((13824, 128), jnp.bfloat16),
            pltpu.VMEM((27, 32, 128), jnp.bfloat16),
            pltpu.VMEM((4, 128, 128), jnp.float32),
            pltpu.VMEM((216, 512), jnp.bfloat16),
            pltpu.VMEM((128, 16, 128), jnp.float32),
            pltpu.VMEM((13824, 128), jnp.float32),
            pltpu.SMEM((tiles, 128), jnp.int32),
            pltpu.VMEM((chunk, 128), jnp.float32),
            pltpu.VMEM((128, chunk), jnp.bfloat16),
            pltpu.VMEM((256, chunk), jnp.float32),
            pltpu.VMEM((256, chunk), jnp.float32),
            pltpu.VMEM((256, 128), jnp.bfloat16),
            pltpu.VMEM((8, chunk), jnp.float32),
            pltpu.VMEM((16, 256), jnp.float32),
            pltpu.VMEM((256, 256), jnp.float32),
            pltpu.SemaphoreType.DMA((copy_count,)),
        ],
        compiler_params=pltpu.CompilerParams(vmem_limit_bytes=48 * 1024 * 1024),
        name="pairs",
    )(rows, first, second, mask, *features, *weights)


def swap(block, axis):
    count = lax.axis_size(axis)
    forward = [(i, (i + 1) % count) for i in range(count)]
    backward = [(target, source) for source, target in forward]
    return lax.ppermute(block, axis, forward), lax.ppermute(block, axis, backward)


def lines():
    length = lax.axis_size("gz")
    up = []
    for x in range(lax.axis_size("gx")):
        for z in range(length):
            target = (x, z + 1) if z + 1 < length else (x ^ 1, 0)
            up.append((x * length + z, target[0] * length + target[1]))
    return up, [(target, source) for source, target in up]


def carry_across(block):
    count = lax.axis_size("gx")
    return lax.ppermute(
        block, "gx", [(i, (i + 2) % count if i % 2 == 0 else (i - 2) % count) for i in range(count)]
    )


def carry_back(block):
    count = lax.axis_size("gx")
    return lax.ppermute(
        block, "gx", [(i, (i - 2) % count if i % 2 == 0 else (i + 2) % count) for i in range(count)]
    )


def collect(brick, prepare):
    up, down = lines()
    line = ("gx", "gz")
    u1 = lax.ppermute(brick, line, up)
    d1 = lax.ppermute(brick, line, down)
    early_low, early_high = swap(jnp.concatenate([brick, u1, d1], axis=0), "gy")
    tied, _ = lax.optimization_barrier((brick, u1))
    prepared = prepare(tied)
    u2 = lax.ppermute(u1, line, up)
    d2 = lax.ppermute(d1, line, down)
    u2, d2, prepared = lax.optimization_barrier((u2, d2, prepared))
    u3 = lax.ppermute(u2, line, up)
    d3 = lax.ppermute(d2, line, down)
    u4 = lax.ppermute(u3[:half_message], line, up)
    d4 = lax.ppermute(d3[half_message:], line, down)
    place = lax.axis_index("gz")
    low = jnp.where(place == 0, u1, d3)
    high = jnp.where(place == lax.axis_size("gz") - 1, d1, u3)
    far = carry_across(jnp.concatenate([low, u4, d4, high], axis=0))
    late_low, late_high = swap(jnp.concatenate([u3, d3, u4, d4], axis=0), "gy")
    far_low, far_high = swap(far, "gy")
    features = (
        (early_low, late_low, far_low)
        + (brick, u1, d1, u3, d3, u4, d4, far)
        + (early_high, late_high, far_high)
    )
    return features, prepared


def block_of(slot):
    step_x = slot // 9 - 1
    step_y = slot // 3 % 3
    step_z = slot % 3 - 1
    place = lax.axis_index("gz")
    bottom = place == 0
    top = place == lax.axis_size("gz") - 1
    partner = 1 - 2 * (lax.axis_index("gx") % 2)
    same = jnp.where(
        step_z == 0, 0, jnp.where(step_z < 0, jnp.where(bottom, 4, 1), jnp.where(top, 3, 2))
    )
    beside = jnp.where(
        step_z == 0, 5, jnp.where(step_z < 0, jnp.where(bottom, 1, 4), jnp.where(top, 2, 3))
    )
    column = jnp.where(
        step_x == 0, same, jnp.where(step_x == partner, beside, 7 + step_z)
    )
    return step_y * 9 + column


def local(
    features,
    positions,
    counts,
    pair_first,
    pair_second,
    pair_mask,
    w_centre,
    w_neighbour,
    w_charge,
    w_radial,
    w_hidden,
    w_energy,
):
    brick = make_brick(
        features[0, 0, 0], positions[0, 0, 0], counts[0, 0], w_charge.reshape(1, -1)
    )
    second_tab = pair_second[0, 0, 0]

    def prepare(tied):
        rows = block_of(second_tab // atoms) * atoms + second_tab % atoms
        weights = arrange(tied, w_centre, w_neighbour, w_radial, w_hidden, w_energy)
        return rows.reshape(-1, tiles, 128), weights

    pieces, (rows, weights) = collect(brick, prepare)
    out_low, out_mid, out_high = pair_sums(
        rows, pair_first[0, 0, 0], second_tab, pair_mask[0, 0, 0], pieces, weights
    )

    def give(low, mid, high, axis):
        count = lax.axis_size(axis)
        forward = [(i, (i + 1) % count) for i in range(count)]
        backward = [(target, source) for source, target in forward]
        return mid + lax.ppermute(high, axis, forward) + lax.ppermute(low, axis, backward)

    plane = give(out_low, out_mid, out_high, "gy")
    even = lax.axis_index("gx") % 2 == 0
    below, centre, above = (plane[x::3] for x in range(3))
    far = carry_back(jnp.where(even, below, above))
    near = jnp.where(even, above, below) + far
    both = jnp.stack([centre, near], axis=0)
    both = give(both[:, 0], both[:, 1], both[:, 2], "gz")
    partners = [(i, i ^ 1) for i in range(lax.axis_size("gx"))]
    summed = (both[0] + lax.ppermute(both[1], "gx", partners)).reshape(4, atoms)
    return (summed[:3][None, None, None], summed[3][None, None, None])


def solution(mesh):
    placed = (
        P("gx", "gy", "gz", None, None),
        P("gx", "gy", "gz", None, None),
        P("gx", "gy", "gz"),
        P("gx", "gy", "gz", None, None),
        P("gx", "gy", "gz", None, None),
        P("gx", "gy", "gz", None, None),
        P(),
        P(),
        P(),
        P(),
        P(),
        P(),
    )
    return jax.shard_map(
        local,
        mesh=mesh,
        in_specs=placed,
        out_specs=(P("gx", "gy", "gz", None, None), P("gx", "gy", "gz", None)),
        check_vma=False,
    )
```

```python
import jax
import jax.numpy as jnp
from jax import lax
from jax.experimental import pallas as pl
from jax.experimental.pallas import tpu as pltpu
from jax.sharding import PartitionSpec as P

delta_sq = 0.04
spread = 0.3
coulomb = 0.2
root_pi = 1.7724538509055159
chunk = 512
tiles = chunk // 128
atoms = 512
message = 544
half_message = message // 2
group = 3 * message
side_bricks = tuple((piece, e * message) for piece in range(3) for e in range(3))
own_bricks = tuple((piece, 0) for piece in range(5)) + (None,) + tuple(
    (7, e * message) for e in range(3)
)


def copy_list():
    features, coords = [], []
    for side, (base, bricks) in enumerate(((0, side_bricks), (3, own_bricks), (11, side_bricks))):
        for e, brick in enumerate(bricks):
            block = side * 9 + e
            at = block * atoms
            if brick is None:
                rest = atoms - half_message
                features.append((base + 5, 0, half_message, at))
                features.append((base + 6, 0, rest, at + half_message))
                coords.append((base + 6, rest, block))
            else:
                piece, begin = brick
                features.append((base + piece, begin, atoms, at))
                coords.append((base + piece, begin + atoms, block))
    return features, coords


piece_count = 14
weight_count = 5
feature_copies, coord_copies = copy_list()
copy_count = len(feature_copies) + len(coord_copies) + weight_count + 1

erfc_p = (
    2.326819970068386e-2, -1.387039388740657e-1, 3.687424674597105e-1, -5.824733027278666e-1,
    6.210004621745983e-1, -4.944515323274145e-1, 3.404879937665872e-1, -2.741127028184656e-1,
    5.638259427386472e-1,
)
erfc_r = (
    -1.047766399936249e1, 1.297719955372516e1, -7.495518717768503e0, 2.921019019210786e0,
    -1.015265279202700e0, 4.218463358204948e-1, -2.820767439740514e-1, 5.641895067754075e-1,
)
erf_t = (
    7.853861353153693e-5, -8.010193625184903e-4, 5.188327685732524e-3, -2.685381193529856e-2,
    1.128358514861418e-1, -3.761262582423300e-1, 1.128379165726710e0,
)


def poly(x, coefficients):
    total = jnp.full_like(x, coefficients[0])
    for value in coefficients[1:]:
        total = total * x + value
    return total


def erfc_positive(x, exp_minus_sq):
    square = x * x
    inverse = 1.0 / square
    tail = exp_minus_sq / x * jnp.where(x < 2.0, poly(inverse, erfc_p), poly(inverse, erfc_r))
    return jnp.where(x < 1.0, 1.0 - x * poly(square, erf_t), tail)


def geometry_phase(
    coords_ref, rows_ref, first_ref, second_ref, mask_ref, out_ref, place_ref, top_ref, iota_ref
):
    rows = 32
    wide = 512
    own = coords_ref[9, 0:16, :].astype(jnp.float32) + coords_ref[9, 16:32, :].astype(
        jnp.float32
    )
    for side in range(3):
        parts = coords_ref[side * 9 : side * 9 + 9].astype(jnp.float32)
        for part in range(2):
            at = part * 16
            block = jnp.concatenate([parts[:, at : at + 8], parts[:, at + 8 : at + 16]], axis=2)
            top_ref[side * 72 : side * 72 + 72, part * 256 : part * 256 + 256] = block.reshape(
                72, 256
            ).astype(jnp.bfloat16)

    def locate(index, carry):
        second = jnp.concatenate(
            [rows_ref[index, k : k + 1, :] for k in range(4)], axis=1
        )
        low = (second & 255).astype(jnp.float32).astype(jnp.bfloat16)
        high = jnp.broadcast_to(second >> 8, (8, wide))
        hot = jnp.where(
            jnp.concatenate([iota_ref[...]] * 4, axis=1) == jnp.broadcast_to(low, (256, wide)),
            jnp.ones((), jnp.bfloat16),
            jnp.zeros((), jnp.bfloat16),
        )
        found = jnp.dot(
            top_ref[...],
            jnp.concatenate([hot, hot], axis=0),
            preferred_element_type=jnp.float32,
        )
        odd = lax.broadcasted_iota(jnp.int32, (8, wide), 0) & 1
        total = jnp.zeros((8, wide), jnp.float32)
        for slot in range(27):
            hit = high == odd + 2 * slot
            total = total + jnp.where(hit, found[slot * 8 : slot * 8 + 8], 0.0)
        for c in range(4):
            row = total[2 * c : 2 * c + 1] + total[2 * c + 1 : 2 * c + 2]
            for k in range(4):
                place_ref[c, pl.ds(index * 4 + k, 1), :] = row[:, k * 128 : k * 128 + 128]
        return carry

    lax.fori_loop(0, 32, locate, 0, unroll=2)

    def group(index, carry):
        base = pl.multiple_of(index * rows, rows)
        first = first_ref[pl.ds(base, rows), :]
        second = second_ref[pl.ds(base, rows), :]
        weight = mask_ref[pl.ds(base, rows), :].astype(jnp.float32)
        lane_i = first & 127
        row_i = first >> 7

        def pick(row, lanes):
            wide = jnp.broadcast_to(row, (rows, 128))
            return jnp.take_along_axis(wide, lanes, axis=1, mode="promise_in_bounds")

        zeros = jnp.zeros((rows, 128), jnp.float32)
        place_j = [place_ref[c, pl.ds(base, rows), :] for c in range(4)]
        place_i = [zeros] * 4
        for part in range(4):
            hit = row_i == part
            for c in range(4):
                at = (part & 1) * 8 + c * 2 + (part >> 1)
                place_i[c] = jnp.where(
                    hit, pick(own[at : at + 1], lane_i), place_i[c]
                )
        slot = second >> 9
        step_x = (slot * 57) >> 9
        rest = slot - step_x * 9
        step_y = (rest * 11) >> 5
        step_z = rest - step_y * 3
        sep = [
            (place_j[c] + (step.astype(jnp.float32) - 1.0)) - place_i[c]
            for c, step in enumerate((step_x, step_y, step_z))
        ]
        dist_sq = sep[0] * sep[0] + sep[1] * sep[1] + sep[2] * sep[2] + delta_sq
        distance = jnp.sqrt(dist_sq)
        inverse = 1.0 / distance
        exp_minus = jnp.exp(-dist_sq)
        screened = erfc_positive(distance, exp_minus)
        potential = screened * inverse
        slope_coul = -(2.0 / root_pi) * exp_minus * inverse - screened / dist_sq
        envelope = jnp.exp(-0.5 * dist_sq)
        values = (
            sep[0],
            sep[1],
            sep[2],
            distance,
            weight * envelope * inverse,
            weight * coulomb * place_i[3] * place_j[3] * slope_coul * inverse,
            weight * coulomb * place_j[3] * potential,
            weight * coulomb * place_i[3] * potential,
            (first & 255).astype(jnp.float32),
            (first >> 8).astype(jnp.float32),
            (second & 255).astype(jnp.float32),
            (second >> 8).astype(jnp.float32),
        )
        for position, value in enumerate(values):
            out_ref[pl.ds(base, rows), position, :] = value
        return carry

    lax.fori_loop(0, 128 // rows, group, 0)
    out_ref[:, 12:16, :] = jnp.zeros((128, 4, 128), jnp.float32)


def brick_kernel(features_ref, positions_ref, counts_ref, charge_ref, out_ref):
    features = features_ref[...]
    weight = jnp.broadcast_to(charge_ref[...], (8, 128))
    raw = lax.dot_general(
        weight, features, (((1,), (1,)), ((), ())), preferred_element_type=jnp.float32
    )[0:1]
    filled = counts_ref[0]
    alive = lax.broadcasted_iota(jnp.int32, (1, atoms), 1) < filled
    total = jnp.sum(jnp.where(alive, raw, 0.0), axis=1, keepdims=True)
    charges = jnp.where(alive, raw - total / filled.astype(jnp.float32), 0.0)
    halves = [positions_ref[c, :, 256 * h : 256 * h + 256] for c in range(3) for h in range(2)]
    halves += [charges[:, 0:256], charges[:, 256:512]]
    coords = jnp.concatenate(halves, axis=0)
    coords = jnp.concatenate([coords[:, 0:128], coords[:, 128:256]], axis=0)
    top = coords.astype(jnp.bfloat16)
    out_ref[0:atoms, :] = features
    out_ref[atoms : atoms + 16, :] = top
    out_ref[atoms + 16 : message, :] = (coords - top.astype(jnp.float32)).astype(jnp.bfloat16)


def make_brick(features, positions, counts, w_charge):
    vmem = pl.BlockSpec(memory_space=pltpu.VMEM)
    return pl.pallas_call(
        brick_kernel,
        out_shape=jax.ShapeDtypeStruct((message, 128), jnp.bfloat16),
        in_specs=[vmem, vmem, pl.BlockSpec(memory_space=pltpu.SMEM), vmem],
        name="brick",
    )(features, positions, counts, w_charge)


def close_kernel(own_ref, partner_ref, forces_ref, charge_ref):
    total = own_ref[...] + partner_ref[...]
    for c in range(4):
        row = jnp.concatenate([total[2 * c : 2 * c + 1], total[2 * c + 1 : 2 * c + 2]], axis=1)
        if c < 3:
            forces_ref[c] = row
        else:
            charge_ref[...] = row


def close(own, partner):
    return pl.pallas_call(
        close_kernel,
        out_shape=(
            jax.ShapeDtypeStruct((3, 1, atoms), jnp.float32),
            jax.ShapeDtypeStruct((1, atoms), jnp.float32),
        ),
        name="close",
    )(own, partner)


def arrange_kernel(
    brick_ref, centre_ref, neighbour_ref, radial_ref, hidden_ref, energy_ref,
    first_out, half_out, turned_out, energy_out, back_out,
):
    centre = lax.dot_general(
        centre_ref[...],
        brick_ref[0:atoms, :],
        (((0,), (1,)), ((), ())),
        preferred_element_type=jnp.float32,
    )
    first_out[:, 0:512] = (centre.astype(jnp.bfloat16).astype(jnp.float32) * 0.5).astype(
        jnp.bfloat16
    )
    first_out[:, 512:640] = (neighbour_ref[...].astype(jnp.float32).T * 0.5).astype(jnp.bfloat16)
    radial = radial_ref[...] * 0.5
    top = radial.astype(jnp.bfloat16).astype(jnp.float32)
    rest = radial - top
    side = jnp.concatenate([top, rest, top, jnp.zeros((104, 256), jnp.float32)], axis=0)
    first_out[:, 640:768] = side.T.astype(jnp.bfloat16)
    hidden = hidden_ref[...].astype(jnp.float32) * 0.5
    half_out[...] = hidden.astype(jnp.bfloat16)
    turned_out[...] = hidden.T.astype(jnp.bfloat16)
    energy_out[...] = jnp.broadcast_to(energy_ref[...], (128, 256)).T
    back_out[...] = jnp.concatenate([top, rest], axis=0).astype(jnp.bfloat16)


def arrange(brick, w_centre, w_neighbour, w_radial, w_hidden, w_energy):
    def shape(rows, columns, kind=jnp.bfloat16):
        return jax.ShapeDtypeStruct((rows, columns), kind)

    return pl.pallas_call(
        arrange_kernel,
        out_shape=(
            shape(256, 768),
            shape(256, 256),
            shape(256, 256),
            shape(256, 128, jnp.float32),
            shape(16, 256),
        ),
        name="arrange",
    )(brick, w_centre, w_neighbour, w_radial, w_hidden, w_energy.reshape(1, -1))


def pair_kernel(rows_ref, pick_first, pick_second, pick_mask, *refs):
    pair_body(
        rows_ref,
        pick_first,
        pick_second,
        pick_mask,
        refs[:piece_count],
        refs[piece_count : piece_count + weight_count],
        *refs[piece_count + weight_count :],
    )


def pair_body(
    rows_ref,
    pick_first,
    pick_second,
    pick_mask,
    sources,
    weights,
    out_low,
    out_mid,
    out_high,
    first_ref,
    hidden_ref,
    hidden_t_ref,
    energy_ref,
    back_ref,
    stage_ref,
    coords_ref,
    place_ref,
    top_ref,
    geo_ref,
    table_ref,
    picks_ref,
    gather_ref,
    feature_ref,
    half_ref,
    slope_ref,
    iota_ref,
    term_ref,
    acc_i_ref,
    acc_j_ref,
    sems,
):
    last = rows_ref.shape[0] - 1

    def picks(index):
        return pltpu.make_async_copy(
            rows_ref.at[jnp.minimum(index, last)], picks_ref, sems.at[copy_count - 1]
        )

    picks(0).start()
    plan = [
        (sources[piece].at[pl.ds(begin, 32)], coords_ref.at[block])
        for piece, begin, block in coord_copies
    ]
    plan += [
        (sources[piece].at[pl.ds(begin, size)], stage_ref.at[pl.ds(at, size)])
        for piece, begin, size, at in feature_copies
    ]
    plan += list(zip(weights, (first_ref, hidden_ref, hidden_t_ref, energy_ref, back_ref)))
    copies = [
        pltpu.make_async_copy(source, target, sems.at[k])
        for k, (source, target) in enumerate(plan)
    ]
    for copy in copies:
        copy.start()
    one = jnp.ones((), jnp.bfloat16)
    zero = jnp.zeros((), jnp.bfloat16)
    iota_ref[...] = (
        lax.broadcasted_iota(jnp.int32, (256, 128), 0).astype(jnp.float32).astype(jnp.bfloat16)
    )
    acc_i_ref[...] = jnp.zeros_like(acc_i_ref)
    acc_j_ref[...] = jnp.zeros_like(acc_j_ref)
    term_ref[...] = jnp.zeros_like(term_ref)
    for copy in copies[: len(coord_copies)]:
        copy.wait()
    geometry_phase(
        coords_ref, rows_ref, pick_first, pick_second, pick_mask, geo_ref, place_ref, top_ref,
        iota_ref,
    )
    tile = lax.broadcasted_iota(jnp.int32, (128, 128), 0) + tiles
    blocks = jnp.max(jnp.where(pick_mask[...] != 0, tile, 0)) // tiles
    for copy in copies[len(coord_copies) :]:
        copy.wait()

    def widen(step, carry):
        rows = pl.ds(pl.multiple_of(step * 256, 256), 256)
        table_ref[rows, :] = stage_ref[rows, :].astype(jnp.float32)
        return carry

    lax.fori_loop(0, 54, widen, 0)

    def fetch(*parts):
        for part in parts or range(tiles):
            for p in range(part * 128, part * 128 + 128):
                row = picks_ref[part, p % 128]
                gather_ref[pl.ds(p, 1), :] = table_ref[pl.ds(row, 1), :]

    def turn():
        feature_ref[...] = gather_ref[...].T.astype(jnp.bfloat16)

    def geo_of(index):
        return jnp.concatenate([geo_ref[index * tiles + k] for k in range(tiles)], axis=1)

    def equal(rows, row):
        width = row.shape[1]
        iota = jnp.concatenate([iota_ref[0:rows, :]] * (width // 128), axis=1)
        return jnp.where(
            iota == jnp.broadcast_to(row.astype(jnp.bfloat16), (rows, width)), one, zero
        )

    def basis_of(distance):
        offset = distance - (
            0.25 + 0.3 * lax.broadcasted_iota(jnp.int32, (8, distance.shape[1]), 0).astype(jnp.float32)
        )
        return offset, jnp.exp(-(offset / spread) * (offset / spread))

    def enter(index):
        geo = geo_of(jnp.minimum(index, last))
        offset, basis = basis_of(geo[3:4])
        top = basis.astype(jnp.bfloat16).astype(jnp.float32)
        low = geo[8:9]
        side = geo[9:10]
        operand = jnp.concatenate(
            [
                equal(256, jnp.where(side == 0.0, low, 512.0)),
                equal(256, jnp.where(side == 0.0, 512.0, low)),
                feature_ref[...],
                jnp.concatenate([top, top, basis - top, jnp.zeros_like(top)], axis=0).astype(
                    jnp.bfloat16
                ),
                jnp.zeros((96, chunk), jnp.bfloat16),
            ],
            axis=0,
        )
        half_ref[...] = jnp.dot(first_ref[...], operand, preferred_element_type=jnp.float32)

    def activate(lanes):
        half_one = half_ref[:, lanes]
        bend_one = jnp.tanh(half_one)
        gain_one = 1.0 + bend_one
        act_one = half_one * gain_one
        slope_ref[:, lanes] = gain_one + act_one * (1.0 - bend_one)
        return jnp.dot(
            hidden_t_ref[...], act_one.astype(jnp.bfloat16), preferred_element_type=jnp.float32
        )

    def second(half_two):
        width = half_two.shape[1]
        bend_two = jnp.tanh(half_two)
        gain_two = 1.0 + bend_two
        act_two = half_two * gain_two
        slope_two = gain_two + act_two * (1.0 - bend_two)
        energy = jnp.concatenate([energy_ref[...]] * (width // 128), axis=1)
        readout = jnp.sum(act_two * energy, axis=0, keepdims=True)
        back_two = (slope_two * energy).astype(jnp.bfloat16)
        return readout, jnp.dot(hidden_ref[...], back_two, preferred_element_type=jnp.float32)

    def finish(index, lanes, readout, back_one):
        geo = geo_of(index)[:, lanes]
        back_one = (back_one * slope_ref[:, lanes]).astype(jnp.bfloat16)
        back_basis = jnp.dot(back_ref[...], back_one, preferred_element_type=jnp.float32)
        distance = geo[3:4]
        offset, basis = basis_of(distance)
        total = jnp.sum(
            (back_basis[0:8] + back_basis[8:16])
            * (basis * offset * (-2.0 / (spread * spread))),
            axis=0,
            keepdims=True,
        ) - (readout * distance)
        push = geo[4:5] * total + geo[5:6]
        term_ref[0:3, lanes] = geo[0:3] * push
        term_ref[3:5, lanes] = geo[6:8]

    def deposit(index):
        geo = geo_of(jnp.maximum(index, 0))
        terms = term_ref[...]
        own = terms[0:4]
        own_top = own.astype(jnp.bfloat16).astype(jnp.float32)
        own_rest = own - own_top
        side = geo[9:10]
        own_rows = jnp.concatenate(
            [
                jnp.where(side == half, part, 0.0)
                for half in (0.0, 1.0)
                for part in (own_top, own_rest)
            ],
            axis=0,
        ).astype(jnp.bfloat16)
        acc_i_ref[...] += lax.dot_general(
            own_rows,
            equal(256, geo[8:9]),
            (((1,), (1,)), ((), ())),
            preferred_element_type=jnp.float32,
        )
        far = jnp.concatenate([-terms[0:3], terms[4:5]], axis=0).astype(jnp.bfloat16)
        hit = equal(64, geo[11:12])
        far_rows = jnp.concatenate(
            [hit * jnp.broadcast_to(far[c : c + 1], (64, chunk)) for c in range(4)], axis=0
        )
        acc_j_ref[...] += lax.dot_general(
            far_rows,
            equal(256, geo[10:11]),
            (((1,), (1,)), ((), ())),
            preferred_element_type=jnp.float32,
        )

    picks(0).wait()
    fetch()
    picks(1).start()
    turn()
    enter(0)
    picks(1).wait()
    fetch()
    picks(2).start()

    def block(index, carry):
        picks(index + 2).wait()
        sides = (slice(0, chunk // 2), slice(chunk // 2, chunk))
        two_a = activate(sides[0])
        two_b = activate(sides[1])
        turn()
        enter(index + 1)
        fetch()
        read_a, back_a = second(two_a)
        deposit(index - 1)
        read_b, back_b = second(two_b)
        finish(index, sides[0], read_a, back_a)
        finish(index, sides[1], read_b, back_b)
        picks(index + 3).start()
        return carry

    lax.fori_loop(0, blocks, block, 0)
    picks(blocks + 2).wait()
    deposit(blocks - 1)
    acc_i = acc_i_ref[...]
    acc_i = jnp.concatenate([acc_i[0:4] + acc_i[4:8], acc_i[8:12] + acc_i[12:16]], axis=0)
    for c in range(4):
        plane = acc_j_ref[c * 64 : c * 64 + 64, :]
        for slot in range(27):
            step_x, step_y, step_z = slot // 9, slot // 3 % 3, slot % 3
            target = (out_low, out_mid, out_high)[step_y]
            for half in range(2):
                row = plane[slot * 2 + half : slot * 2 + half + 1]
                if slot == 13:
                    row = row + acc_i[half * 4 + c : half * 4 + c + 1]
                target[step_z * 3 + step_x, c * 2 + half : c * 2 + half + 1, :] = row


def pair_sums(rows, first, second, mask, features, weights):
    vmem = pl.BlockSpec(memory_space=pltpu.VMEM)
    far = pl.BlockSpec(memory_space=pltpu.HBM)
    out = jax.ShapeDtypeStruct((9, 8, 256), jnp.float32)
    return pl.pallas_call(
        pair_kernel,
        out_shape=(out, out, out),
        in_specs=[vmem] * 4 + [far] * (piece_count + weight_count),
        out_specs=(vmem, vmem, vmem),
        scratch_shapes=[
            pltpu.VMEM((256, 768), jnp.bfloat16),
            pltpu.VMEM((256, 256), jnp.bfloat16),
            pltpu.VMEM((256, 256), jnp.bfloat16),
            pltpu.VMEM((256, 128), jnp.float32),
            pltpu.VMEM((16, 256), jnp.bfloat16),
            pltpu.VMEM((13824, 128), jnp.bfloat16),
            pltpu.VMEM((27, 32, 128), jnp.bfloat16),
            pltpu.VMEM((4, 128, 128), jnp.float32),
            pltpu.VMEM((216, 512), jnp.bfloat16),
            pltpu.VMEM((128, 16, 128), jnp.float32),
            pltpu.VMEM((13824, 128), jnp.float32),
            pltpu.SMEM((tiles, 128), jnp.int32),
            pltpu.VMEM((chunk, 128), jnp.float32),
            pltpu.VMEM((128, chunk), jnp.bfloat16),
            pltpu.VMEM((256, chunk), jnp.float32),
            pltpu.VMEM((256, chunk), jnp.float32),
            pltpu.VMEM((256, 128), jnp.bfloat16),
            pltpu.VMEM((8, chunk), jnp.float32),
            pltpu.VMEM((16, 256), jnp.float32),
            pltpu.VMEM((256, 256), jnp.float32),
            pltpu.SemaphoreType.DMA((copy_count,)),
        ],
        compiler_params=pltpu.CompilerParams(vmem_limit_bytes=48 * 1024 * 1024),
        name="pairs",
    )(rows, first, second, mask, *features, *weights)


def swap(block, axis):
    count = lax.axis_size(axis)
    forward = [(i, (i + 1) % count) for i in range(count)]
    backward = [(target, source) for source, target in forward]
    return lax.ppermute(block, axis, forward), lax.ppermute(block, axis, backward)


def lines():
    length = lax.axis_size("gz")
    up = []
    for x in range(lax.axis_size("gx")):
        for z in range(length):
            target = (x, z + 1) if z + 1 < length else (x ^ 1, 0)
            up.append((x * length + z, target[0] * length + target[1]))
    return up, [(target, source) for source, target in up]


def carry_across(block):
    count = lax.axis_size("gx")
    return lax.ppermute(
        block, "gx", [(i, (i + 2) % count if i % 2 == 0 else (i - 2) % count) for i in range(count)]
    )


def carry_back(block):
    count = lax.axis_size("gx")
    return lax.ppermute(
        block, "gx", [(i, (i - 2) % count if i % 2 == 0 else (i + 2) % count) for i in range(count)]
    )


def collect(brick, prepare):
    up, down = lines()
    line = ("gx", "gz")
    u1 = lax.ppermute(brick, line, up)
    d1 = lax.ppermute(brick, line, down)
    early_low, early_high = swap(jnp.concatenate([brick, u1, d1], axis=0), "gy")
    tied, _ = lax.optimization_barrier((brick, u1))
    prepared = prepare(tied)
    u2 = lax.ppermute(u1, line, up)
    d2 = lax.ppermute(d1, line, down)
    u2, d2, prepared = lax.optimization_barrier((u2, d2, prepared))
    u3 = lax.ppermute(u2, line, up)
    d3 = lax.ppermute(d2, line, down)
    u4 = lax.ppermute(u3[:half_message], line, up)
    d4 = lax.ppermute(d3[half_message:], line, down)
    place = lax.axis_index("gz")
    low = jnp.where(place == 0, u1, d3)
    high = jnp.where(place == lax.axis_size("gz") - 1, d1, u3)
    far = carry_across(jnp.concatenate([low, u4, d4, high], axis=0))
    late_low, late_high = swap(jnp.concatenate([u3, d3, u4, d4], axis=0), "gy")
    far_low, far_high = swap(far, "gy")
    features = (
        (early_low, late_low, far_low)
        + (brick, u1, d1, u3, d3, u4, d4, far)
        + (early_high, late_high, far_high)
    )
    return features, prepared


def block_of(slot):
    step_x = slot // 9 - 1
    step_y = slot // 3 % 3
    step_z = slot % 3 - 1
    place = lax.axis_index("gz")
    bottom = place == 0
    top = place == lax.axis_size("gz") - 1
    partner = 1 - 2 * (lax.axis_index("gx") % 2)
    same = jnp.where(
        step_z == 0, 0, jnp.where(step_z < 0, jnp.where(bottom, 4, 1), jnp.where(top, 3, 2))
    )
    beside = jnp.where(
        step_z == 0, 5, jnp.where(step_z < 0, jnp.where(bottom, 1, 4), jnp.where(top, 2, 3))
    )
    column = jnp.where(
        step_x == 0, same, jnp.where(step_x == partner, beside, 7 + step_z)
    )
    return step_y * 9 + column


def local(
    features,
    positions,
    counts,
    pair_first,
    pair_second,
    pair_mask,
    w_centre,
    w_neighbour,
    w_charge,
    w_radial,
    w_hidden,
    w_energy,
):
    brick = make_brick(
        features[0, 0, 0], positions[0, 0, 0][:, None, :], counts[0, 0], w_charge.reshape(1, -1)
    )
    second_tab = pair_second[0, 0, 0]

    def prepare(tied):
        rows = block_of(second_tab // atoms) * atoms + second_tab % atoms
        weights = arrange(tied, w_centre, w_neighbour, w_radial, w_hidden, w_energy)
        return rows.reshape(-1, tiles, 128), weights

    pieces, (rows, weights) = collect(brick, prepare)
    out_low, out_mid, out_high = pair_sums(
        rows, pair_first[0, 0, 0], second_tab, pair_mask[0, 0, 0], pieces, weights
    )

    def give(low, mid, high, axis):
        count = lax.axis_size(axis)
        forward = [(i, (i + 1) % count) for i in range(count)]
        backward = [(target, source) for source, target in forward]
        return mid + lax.ppermute(high, axis, forward) + lax.ppermute(low, axis, backward)

    plane = give(out_low, out_mid, out_high, "gy")
    even = lax.axis_index("gx") % 2 == 0
    below, centre, above = (plane[x::3] for x in range(3))
    far = carry_back(jnp.where(even, below, above))
    near = jnp.where(even, above, below) + far
    both = jnp.stack([centre, near], axis=0)
    both = give(both[:, 0], both[:, 1], both[:, 2], "gz")
    partners = [(i, i ^ 1) for i in range(lax.axis_size("gx"))]
    forces, charge_grad = close(both[0], lax.ppermute(both[1], "gx", partners))
    return (forces.reshape(1, 1, 1, 3, atoms), charge_grad.reshape(1, 1, 1, atoms))


def solution(mesh):
    placed = (
        P("gx", "gy", "gz", None, None),
        P("gx", "gy", "gz", None, None),
        P("gx", "gy", "gz"),
        P("gx", "gy", "gz", None, None),
        P("gx", "gy", "gz", None, None),
        P("gx", "gy", "gz", None, None),
        P(),
        P(),
        P(),
        P(),
        P(),
        P(),
    )
    return jax.shard_map(
        local,
        mesh=mesh,
        in_specs=placed,
        out_specs=(P("gx", "gy", "gz", None, None), P("gx", "gy", "gz", None)),
        check_vma=False,
    )
```

```python
import jax
import jax.numpy as jnp
from jax import lax
from jax.experimental import pallas as pl
from jax.experimental.pallas import tpu as pltpu
from jax.sharding import PartitionSpec as P

delta_sq = 0.04
spread = 0.3
coulomb = 0.2
root_pi = 1.7724538509055159
chunk = 512
tiles = chunk // 128
atoms = 512
message = 544
half_message = message // 2
group = 3 * message
side_bricks = tuple((piece, e * message) for piece in range(3) for e in range(3))
own_bricks = tuple((piece, 0) for piece in range(5)) + (None,) + tuple(
    (7, e * message) for e in range(3)
)


def copy_list():
    features, coords = [], []
    for side, (base, bricks) in enumerate(((0, side_bricks), (3, own_bricks), (11, side_bricks))):
        for e, brick in enumerate(bricks):
            block = side * 9 + e
            at = block * atoms
            if brick is None:
                rest = atoms - half_message
                features.append((base + 5, 0, half_message, at))
                features.append((base + 6, 0, rest, at + half_message))
                coords.append((base + 6, rest, block))
            else:
                piece, begin = brick
                features.append((base + piece, begin, atoms, at))
                coords.append((base + piece, begin + atoms, block))
    return features, coords


piece_count = 14
weight_count = 5
feature_copies, coord_copies = copy_list()
copy_count = len(feature_copies) + len(coord_copies) + weight_count + 1

erfc_p = (
    2.326819970068386e-2, -1.387039388740657e-1, 3.687424674597105e-1, -5.824733027278666e-1,
    6.210004621745983e-1, -4.944515323274145e-1, 3.404879937665872e-1, -2.741127028184656e-1,
    5.638259427386472e-1,
)
erfc_r = (
    -1.047766399936249e1, 1.297719955372516e1, -7.495518717768503e0, 2.921019019210786e0,
    -1.015265279202700e0, 4.218463358204948e-1, -2.820767439740514e-1, 5.641895067754075e-1,
)
erf_t = (
    7.853861353153693e-5, -8.010193625184903e-4, 5.188327685732524e-3, -2.685381193529856e-2,
    1.128358514861418e-1, -3.761262582423300e-1, 1.128379165726710e0,
)


def poly(x, coefficients):
    total = jnp.full_like(x, coefficients[0])
    for value in coefficients[1:]:
        total = total * x + value
    return total


def erfc_positive(x, exp_minus_sq):
    square = x * x
    inverse = 1.0 / square
    tail = exp_minus_sq / x * jnp.where(x < 2.0, poly(inverse, erfc_p), poly(inverse, erfc_r))
    return jnp.where(x < 1.0, 1.0 - x * poly(square, erf_t), tail)


def geometry_phase(
    coords_ref, rows_ref, first_ref, second_ref, mask_ref, out_ref, place_ref, top_ref, iota_ref
):
    rows = 32
    wide = 512
    own = coords_ref[9, 0:16, :].astype(jnp.float32) + coords_ref[9, 16:32, :].astype(
        jnp.float32
    )
    for side in range(3):
        parts = coords_ref[side * 9 : side * 9 + 9].astype(jnp.float32)
        for part in range(2):
            at = part * 16
            block = jnp.concatenate([parts[:, at : at + 8], parts[:, at + 8 : at + 16]], axis=2)
            top_ref[side * 72 : side * 72 + 72, part * 256 : part * 256 + 256] = block.reshape(
                72, 256
            ).astype(jnp.bfloat16)

    def locate(index, carry):
        second = jnp.concatenate(
            [rows_ref[index, k : k + 1, :] for k in range(4)], axis=1
        )
        low = (second & 255).astype(jnp.float32).astype(jnp.bfloat16)
        high = jnp.broadcast_to(second >> 8, (8, wide))
        hot = jnp.where(
            jnp.concatenate([iota_ref[...]] * 4, axis=1) == jnp.broadcast_to(low, (256, wide)),
            jnp.ones((), jnp.bfloat16),
            jnp.zeros((), jnp.bfloat16),
        )
        found = jnp.dot(
            top_ref[...],
            jnp.concatenate([hot, hot], axis=0),
            preferred_element_type=jnp.float32,
        )
        odd = lax.broadcasted_iota(jnp.int32, (8, wide), 0) & 1
        total = jnp.zeros((8, wide), jnp.float32)
        for slot in range(27):
            hit = high == odd + 2 * slot
            total = total + jnp.where(hit, found[slot * 8 : slot * 8 + 8], 0.0)
        for c in range(4):
            row = total[2 * c : 2 * c + 1] + total[2 * c + 1 : 2 * c + 2]
            for k in range(4):
                place_ref[c, pl.ds(index * 4 + k, 1), :] = row[:, k * 128 : k * 128 + 128]
        return carry

    lax.fori_loop(0, 32, locate, 0, unroll=2)

    def group(index, carry):
        base = pl.multiple_of(index * rows, rows)
        first = first_ref[pl.ds(base, rows), :]
        second = second_ref[pl.ds(base, rows), :]
        weight = mask_ref[pl.ds(base, rows), :].astype(jnp.float32)
        lane_i = first & 127
        row_i = first >> 7

        def pick(row, lanes):
            wide = jnp.broadcast_to(row, (rows, 128))
            return jnp.take_along_axis(wide, lanes, axis=1, mode="promise_in_bounds")

        zeros = jnp.zeros((rows, 128), jnp.float32)
        place_j = [place_ref[c, pl.ds(base, rows), :] for c in range(4)]
        place_i = [zeros] * 4
        for part in range(4):
            hit = row_i == part
            for c in range(4):
                at = (part & 1) * 8 + c * 2 + (part >> 1)
                place_i[c] = jnp.where(
                    hit, pick(own[at : at + 1], lane_i), place_i[c]
                )
        slot = second >> 9
        step_x = (slot * 57) >> 9
        rest = slot - step_x * 9
        step_y = (rest * 11) >> 5
        step_z = rest - step_y * 3
        sep = [
            (place_j[c] + (step.astype(jnp.float32) - 1.0)) - place_i[c]
            for c, step in enumerate((step_x, step_y, step_z))
        ]
        dist_sq = sep[0] * sep[0] + sep[1] * sep[1] + sep[2] * sep[2] + delta_sq
        distance = jnp.sqrt(dist_sq)
        inverse = 1.0 / distance
        exp_minus = jnp.exp(-dist_sq)
        screened = erfc_positive(distance, exp_minus)
        potential = screened * inverse
        slope_coul = -(2.0 / root_pi) * exp_minus * inverse - screened / dist_sq
        envelope = jnp.exp(-0.5 * dist_sq)
        values = (
            sep[0],
            sep[1],
            sep[2],
            distance,
            weight * envelope * inverse,
            weight * coulomb * place_i[3] * place_j[3] * slope_coul * inverse,
            weight * coulomb * place_j[3] * potential,
            weight * coulomb * place_i[3] * potential,
            (first & 255).astype(jnp.float32),
            (first >> 8).astype(jnp.float32),
            (second & 255).astype(jnp.float32),
            (second >> 8).astype(jnp.float32),
        )
        for position, value in enumerate(values):
            out_ref[pl.ds(base, rows), position, :] = value
        return carry

    lax.fori_loop(0, 128 // rows, group, 0)
    out_ref[:, 12:16, :] = jnp.zeros((128, 4, 128), jnp.float32)


def brick_kernel(features_ref, positions_ref, counts_ref, charge_ref, out_ref):
    features = features_ref[...]
    weight = jnp.broadcast_to(charge_ref[...], (8, 128))
    raw = lax.dot_general(
        weight, features, (((1,), (1,)), ((), ())), preferred_element_type=jnp.float32
    )[0:1]
    filled = counts_ref[0]
    alive = lax.broadcasted_iota(jnp.int32, (1, atoms), 1) < filled
    total = jnp.sum(jnp.where(alive, raw, 0.0), axis=1, keepdims=True)
    charges = jnp.where(alive, raw - total / filled.astype(jnp.float32), 0.0)
    halves = [positions_ref[c, :, 256 * h : 256 * h + 256] for c in range(3) for h in range(2)]
    halves += [charges[:, 0:256], charges[:, 256:512]]
    coords = jnp.concatenate(halves, axis=0)
    coords = jnp.concatenate([coords[:, 0:128], coords[:, 128:256]], axis=0)
    top = coords.astype(jnp.bfloat16)
    out_ref[0:atoms, :] = features
    out_ref[atoms : atoms + 16, :] = top
    out_ref[atoms + 16 : message, :] = (coords - top.astype(jnp.float32)).astype(jnp.bfloat16)


def make_brick(features, positions, counts, w_charge):
    vmem = pl.BlockSpec(memory_space=pltpu.VMEM)
    return pl.pallas_call(
        brick_kernel,
        out_shape=jax.ShapeDtypeStruct((message, 128), jnp.bfloat16),
        in_specs=[vmem, vmem, pl.BlockSpec(memory_space=pltpu.SMEM), vmem],
        name="brick",
    )(features, positions, counts, w_charge)


def arrange_kernel(
    brick_ref, centre_ref, neighbour_ref, radial_ref, hidden_ref, energy_ref,
    first_out, half_out, turned_out, energy_out, back_out,
):
    centre = lax.dot_general(
        centre_ref[...],
        brick_ref[0:atoms, :],
        (((0,), (1,)), ((), ())),
        preferred_element_type=jnp.float32,
    )
    first_out[:, 0:512] = (centre.astype(jnp.bfloat16).astype(jnp.float32) * 0.5).astype(
        jnp.bfloat16
    )
    first_out[:, 512:640] = (neighbour_ref[...].astype(jnp.float32).T * 0.5).astype(jnp.bfloat16)
    radial = radial_ref[...] * 0.5
    top = radial.astype(jnp.bfloat16).astype(jnp.float32)
    rest = radial - top
    side = jnp.concatenate([top, rest, top, jnp.zeros((104, 256), jnp.float32)], axis=0)
    first_out[:, 640:768] = side.T.astype(jnp.bfloat16)
    hidden = hidden_ref[...].astype(jnp.float32) * 0.5
    half_out[...] = hidden.astype(jnp.bfloat16)
    turned_out[...] = hidden.T.astype(jnp.bfloat16)
    energy_out[...] = jnp.broadcast_to(energy_ref[...], (128, 256)).T
    back_out[...] = jnp.concatenate([top, rest], axis=0).astype(jnp.bfloat16)


def arrange(brick, w_centre, w_neighbour, w_radial, w_hidden, w_energy):
    def shape(rows, columns, kind=jnp.bfloat16):
        return jax.ShapeDtypeStruct((rows, columns), kind)

    return pl.pallas_call(
        arrange_kernel,
        out_shape=(
            shape(256, 768),
            shape(256, 256),
            shape(256, 256),
            shape(256, 128, jnp.float32),
            shape(16, 256),
        ),
        name="arrange",
    )(brick, w_centre, w_neighbour, w_radial, w_hidden, w_energy.reshape(1, -1))


def pair_kernel(rows_ref, pick_first, pick_second, pick_mask, *refs):
    pair_body(
        rows_ref,
        pick_first,
        pick_second,
        pick_mask,
        refs[:piece_count],
        refs[piece_count : piece_count + weight_count],
        *refs[piece_count + weight_count :],
    )


def pair_body(
    rows_ref,
    pick_first,
    pick_second,
    pick_mask,
    sources,
    weights,
    out_low,
    out_mid,
    out_high,
    first_ref,
    hidden_ref,
    hidden_t_ref,
    energy_ref,
    back_ref,
    stage_ref,
    coords_ref,
    place_ref,
    top_ref,
    geo_ref,
    table_ref,
    picks_ref,
    gather_ref,
    feature_ref,
    half_ref,
    slope_ref,
    iota_ref,
    term_ref,
    acc_i_ref,
    acc_j_ref,
    sems,
):
    last = rows_ref.shape[0] - 1

    def picks(index):
        return pltpu.make_async_copy(
            rows_ref.at[jnp.minimum(index, last)], picks_ref, sems.at[copy_count - 1]
        )

    picks(0).start()
    plan = [
        (sources[piece].at[pl.ds(begin, 32)], coords_ref.at[block])
        for piece, begin, block in coord_copies
    ]
    plan += [
        (sources[piece].at[pl.ds(begin, size)], stage_ref.at[pl.ds(at, size)])
        for piece, begin, size, at in feature_copies
    ]
    plan += list(zip(weights, (first_ref, hidden_ref, hidden_t_ref, energy_ref, back_ref)))
    copies = [
        pltpu.make_async_copy(source, target, sems.at[k])
        for k, (source, target) in enumerate(plan)
    ]
    for copy in copies:
        copy.start()
    one = jnp.ones((), jnp.bfloat16)
    zero = jnp.zeros((), jnp.bfloat16)
    iota_ref[...] = (
        lax.broadcasted_iota(jnp.int32, (256, 128), 0).astype(jnp.float32).astype(jnp.bfloat16)
    )
    acc_i_ref[...] = jnp.zeros_like(acc_i_ref)
    acc_j_ref[...] = jnp.zeros_like(acc_j_ref)
    term_ref[...] = jnp.zeros_like(term_ref)
    for copy in copies[: len(coord_copies)]:
        copy.wait()
    geometry_phase(
        coords_ref, rows_ref, pick_first, pick_second, pick_mask, geo_ref, place_ref, top_ref,
        iota_ref,
    )
    tile = lax.broadcasted_iota(jnp.int32, (128, 128), 0) + tiles
    blocks = jnp.max(jnp.where(pick_mask[...] != 0, tile, 0)) // tiles
    for copy in copies[len(coord_copies) :]:
        copy.wait()

    def widen(step, carry):
        rows = pl.ds(pl.multiple_of(step * 256, 256), 256)
        table_ref[rows, :] = stage_ref[rows, :].astype(jnp.float32)
        return carry

    lax.fori_loop(0, 54, widen, 0)

    def fetch(*parts):
        for part in parts or range(tiles):
            for p in range(part * 128, part * 128 + 128):
                row = picks_ref[part, p % 128]
                gather_ref[pl.ds(p, 1), :] = table_ref[pl.ds(row, 1), :]

    def turn():
        feature_ref[...] = gather_ref[...].T.astype(jnp.bfloat16)

    def geo_of(index):
        return jnp.concatenate([geo_ref[index * tiles + k] for k in range(tiles)], axis=1)

    def equal(rows, row):
        width = row.shape[1]
        iota = jnp.concatenate([iota_ref[0:rows, :]] * (width // 128), axis=1)
        return jnp.where(
            iota == jnp.broadcast_to(row.astype(jnp.bfloat16), (rows, width)), one, zero
        )

    def basis_of(distance):
        offset = distance - (
            0.25 + 0.3 * lax.broadcasted_iota(jnp.int32, (8, distance.shape[1]), 0).astype(jnp.float32)
        )
        return offset, jnp.exp(-(offset / spread) * (offset / spread))

    def enter(index):
        geo = geo_of(jnp.minimum(index, last))
        offset, basis = basis_of(geo[3:4])
        top = basis.astype(jnp.bfloat16).astype(jnp.float32)
        low = geo[8:9]
        side = geo[9:10]
        operand = jnp.concatenate(
            [
                equal(256, jnp.where(side == 0.0, low, 512.0)),
                equal(256, jnp.where(side == 0.0, 512.0, low)),
                feature_ref[...],
                jnp.concatenate([top, top, basis - top, jnp.zeros_like(top)], axis=0).astype(
                    jnp.bfloat16
                ),
                jnp.zeros((96, chunk), jnp.bfloat16),
            ],
            axis=0,
        )
        half_ref[...] = jnp.dot(first_ref[...], operand, preferred_element_type=jnp.float32)

    def activate(lanes):
        half_one = half_ref[:, lanes]
        bend_one = jnp.tanh(half_one)
        gain_one = 1.0 + bend_one
        act_one = half_one * gain_one
        slope_ref[:, lanes] = gain_one + act_one * (1.0 - bend_one)
        return jnp.dot(
            hidden_t_ref[...], act_one.astype(jnp.bfloat16), preferred_element_type=jnp.float32
        )

    def second(half_two):
        width = half_two.shape[1]
        bend_two = jnp.tanh(half_two)
        gain_two = 1.0 + bend_two
        act_two = half_two * gain_two
        slope_two = gain_two + act_two * (1.0 - bend_two)
        energy = jnp.concatenate([energy_ref[...]] * (width // 128), axis=1)
        readout = jnp.sum(act_two * energy, axis=0, keepdims=True)
        back_two = (slope_two * energy).astype(jnp.bfloat16)
        return readout, jnp.dot(hidden_ref[...], back_two, preferred_element_type=jnp.float32)

    def finish(index, lanes, readout, back_one):
        geo = geo_of(index)[:, lanes]
        back_one = (back_one * slope_ref[:, lanes]).astype(jnp.bfloat16)
        back_basis = jnp.dot(back_ref[...], back_one, preferred_element_type=jnp.float32)
        distance = geo[3:4]
        offset, basis = basis_of(distance)
        total = jnp.sum(
            (back_basis[0:8] + back_basis[8:16])
            * (basis * offset * (-2.0 / (spread * spread))),
            axis=0,
            keepdims=True,
        ) - (readout * distance)
        push = geo[4:5] * total + geo[5:6]
        term_ref[0:3, lanes] = geo[0:3] * push
        term_ref[3:5, lanes] = geo[6:8]

    def deposit(index):
        geo = geo_of(jnp.maximum(index, 0))
        terms = term_ref[...]
        own = terms[0:4]
        own_top = own.astype(jnp.bfloat16).astype(jnp.float32)
        own_rest = own - own_top
        side = geo[9:10]
        own_rows = jnp.concatenate(
            [
                jnp.where(side == half, part, 0.0)
                for half in (0.0, 1.0)
                for part in (own_top, own_rest)
            ],
            axis=0,
        ).astype(jnp.bfloat16)
        acc_i_ref[...] += lax.dot_general(
            own_rows,
            equal(256, geo[8:9]),
            (((1,), (1,)), ((), ())),
            preferred_element_type=jnp.float32,
        )
        far = jnp.concatenate([-terms[0:3], terms[4:5]], axis=0).astype(jnp.bfloat16)
        hit = equal(64, geo[11:12])
        far_rows = jnp.concatenate(
            [hit * jnp.broadcast_to(far[c : c + 1], (64, chunk)) for c in range(4)], axis=0
        )
        acc_j_ref[...] += lax.dot_general(
            far_rows,
            equal(256, geo[10:11]),
            (((1,), (1,)), ((), ())),
            preferred_element_type=jnp.float32,
        )

    picks(0).wait()
    fetch()
    picks(1).start()
    turn()
    enter(0)
    picks(1).wait()
    fetch()
    picks(2).start()

    def block(index, carry):
        picks(index + 2).wait()
        sides = (slice(0, chunk // 2), slice(chunk // 2, chunk))
        two_a = activate(sides[0])
        two_b = activate(sides[1])
        turn()
        enter(index + 1)
        fetch()
        read_a, back_a = second(two_a)
        deposit(index - 1)
        read_b, back_b = second(two_b)
        finish(index, sides[0], read_a, back_a)
        finish(index, sides[1], read_b, back_b)
        picks(index + 3).start()
        return carry

    lax.fori_loop(0, blocks, block, 0)
    picks(blocks + 2).wait()
    deposit(blocks - 1)
    acc_i = acc_i_ref[...]
    acc_i = jnp.concatenate([acc_i[0:4] + acc_i[4:8], acc_i[8:12] + acc_i[12:16]], axis=0)
    for c in range(4):
        plane = acc_j_ref[c * 64 : c * 64 + 64, :]
        for slot in range(27):
            step_x, step_y, step_z = slot // 9, slot // 3 % 3, slot % 3
            target = (out_low, out_mid, out_high)[step_y]
            for half in range(2):
                row = plane[slot * 2 + half : slot * 2 + half + 1]
                if slot == 13:
                    row = row + acc_i[half * 4 + c : half * 4 + c + 1]
                target[step_z * 3 + step_x, c * 2 + half : c * 2 + half + 1, :] = row


def pair_sums(rows, first, second, mask, features, weights):
    vmem = pl.BlockSpec(memory_space=pltpu.VMEM)
    far = pl.BlockSpec(memory_space=pltpu.HBM)
    out = jax.ShapeDtypeStruct((9, 8, 256), jnp.float32)
    return pl.pallas_call(
        pair_kernel,
        out_shape=(out, out, out),
        in_specs=[vmem] * 4 + [far] * (piece_count + weight_count),
        out_specs=(vmem, vmem, vmem),
        scratch_shapes=[
            pltpu.VMEM((256, 768), jnp.bfloat16),
            pltpu.VMEM((256, 256), jnp.bfloat16),
            pltpu.VMEM((256, 256), jnp.bfloat16),
            pltpu.VMEM((256, 128), jnp.float32),
            pltpu.VMEM((16, 256), jnp.bfloat16),
            pltpu.VMEM((13824, 128), jnp.bfloat16),
            pltpu.VMEM((27, 32, 128), jnp.bfloat16),
            pltpu.VMEM((4, 128, 128), jnp.float32),
            pltpu.VMEM((216, 512), jnp.bfloat16),
            pltpu.VMEM((128, 16, 128), jnp.float32),
            pltpu.VMEM((13824, 128), jnp.float32),
            pltpu.SMEM((tiles, 128), jnp.int32),
            pltpu.VMEM((chunk, 128), jnp.float32),
            pltpu.VMEM((128, chunk), jnp.bfloat16),
            pltpu.VMEM((256, chunk), jnp.float32),
            pltpu.VMEM((256, chunk), jnp.float32),
            pltpu.VMEM((256, 128), jnp.bfloat16),
            pltpu.VMEM((8, chunk), jnp.float32),
            pltpu.VMEM((16, 256), jnp.float32),
            pltpu.VMEM((256, 256), jnp.float32),
            pltpu.SemaphoreType.DMA((copy_count,)),
        ],
        compiler_params=pltpu.CompilerParams(vmem_limit_bytes=48 * 1024 * 1024),
        name="pairs",
    )(rows, first, second, mask, *features, *weights)


def swap(block, axis):
    count = lax.axis_size(axis)
    forward = [(i, (i + 1) % count) for i in range(count)]
    backward = [(target, source) for source, target in forward]
    return lax.ppermute(block, axis, forward), lax.ppermute(block, axis, backward)


def lines():
    length = lax.axis_size("gz")
    up = []
    for x in range(lax.axis_size("gx")):
        for z in range(length):
            target = (x, z + 1) if z + 1 < length else (x ^ 1, 0)
            up.append((x * length + z, target[0] * length + target[1]))
    return up, [(target, source) for source, target in up]


def carry_across(block):
    count = lax.axis_size("gx")
    return lax.ppermute(
        block, "gx", [(i, (i + 2) % count if i % 2 == 0 else (i - 2) % count) for i in range(count)]
    )


def carry_back(block):
    count = lax.axis_size("gx")
    return lax.ppermute(
        block, "gx", [(i, (i - 2) % count if i % 2 == 0 else (i + 2) % count) for i in range(count)]
    )


def collect(brick, prepare):
    up, down = lines()
    line = ("gx", "gz")
    u1 = lax.ppermute(brick, line, up)
    d1 = lax.ppermute(brick, line, down)
    early_low, early_high = swap(jnp.concatenate([brick, u1, d1], axis=0), "gy")
    tied, _ = lax.optimization_barrier((brick, u1))
    prepared = prepare(tied)
    u2 = lax.ppermute(u1, line, up)
    d2 = lax.ppermute(d1, line, down)
    u2, d2, prepared = lax.optimization_barrier((u2, d2, prepared))
    u3 = lax.ppermute(u2, line, up)
    d3 = lax.ppermute(d2, line, down)
    u4 = lax.ppermute(u3[:half_message], line, up)
    d4 = lax.ppermute(d3[half_message:], line, down)
    place = lax.axis_index("gz")
    low = jnp.where(place == 0, u1, d3)
    high = jnp.where(place == lax.axis_size("gz") - 1, d1, u3)
    far = carry_across(jnp.concatenate([low, u4, d4, high], axis=0))
    late_low, late_high = swap(jnp.concatenate([u3, d3, u4, d4], axis=0), "gy")
    far_low, far_high = swap(far, "gy")
    features = (
        (early_low, late_low, far_low)
        + (brick, u1, d1, u3, d3, u4, d4, far)
        + (early_high, late_high, far_high)
    )
    return features, prepared


def block_of(slot):
    step_x = slot // 9 - 1
    step_y = slot // 3 % 3
    step_z = slot % 3 - 1
    place = lax.axis_index("gz")
    bottom = place == 0
    top = place == lax.axis_size("gz") - 1
    partner = 1 - 2 * (lax.axis_index("gx") % 2)
    same = jnp.where(
        step_z == 0, 0, jnp.where(step_z < 0, jnp.where(bottom, 4, 1), jnp.where(top, 3, 2))
    )
    beside = jnp.where(
        step_z == 0, 5, jnp.where(step_z < 0, jnp.where(bottom, 1, 4), jnp.where(top, 2, 3))
    )
    column = jnp.where(
        step_x == 0, same, jnp.where(step_x == partner, beside, 7 + step_z)
    )
    return step_y * 9 + column


def local(
    features,
    positions,
    counts,
    pair_first,
    pair_second,
    pair_mask,
    w_centre,
    w_neighbour,
    w_charge,
    w_radial,
    w_hidden,
    w_energy,
):
    brick = make_brick(
        features[0, 0, 0], positions[0, 0, 0][:, None, :], counts[0, 0], w_charge.reshape(1, -1)
    )
    second_tab = pair_second[0, 0, 0]

    def prepare(tied):
        rows = block_of(second_tab // atoms) * atoms + second_tab % atoms
        weights = arrange(tied, w_centre, w_neighbour, w_radial, w_hidden, w_energy)
        return rows.reshape(-1, tiles, 128), weights

    pieces, (rows, weights) = collect(brick, prepare)
    out_low, out_mid, out_high = pair_sums(
        rows, pair_first[0, 0, 0], second_tab, pair_mask[0, 0, 0], pieces, weights
    )

    def give(low, mid, high, axis):
        count = lax.axis_size(axis)
        forward = [(i, (i + 1) % count) for i in range(count)]
        backward = [(target, source) for source, target in forward]
        return mid + lax.ppermute(high, axis, forward) + lax.ppermute(low, axis, backward)

    plane = give(out_low, out_mid, out_high, "gy")
    even = lax.axis_index("gx") % 2 == 0
    below, centre, above = (plane[x::3] for x in range(3))
    far = carry_back(jnp.where(even, below, above))
    near = jnp.where(even, above, below) + far
    both = jnp.stack([centre, near], axis=0)
    both = give(both[:, 0], both[:, 1], both[:, 2], "gz")
    partners = [(i, i ^ 1) for i in range(lax.axis_size("gx"))]
    summed = (both[0] + lax.ppermute(both[1], "gx", partners)).reshape(4, atoms)
    return (summed[:3][None, None, None], summed[3][None, None, None])


def solution(mesh):
    placed = (
        P("gx", "gy", "gz", None, None),
        P("gx", "gy", "gz", None, None),
        P("gx", "gy", "gz"),
        P("gx", "gy", "gz", None, None),
        P("gx", "gy", "gz", None, None),
        P("gx", "gy", "gz", None, None),
        P(),
        P(),
        P(),
        P(),
        P(),
        P(),
    )
    return jax.shard_map(
        local,
        mesh=mesh,
        in_specs=placed,
        out_specs=(P("gx", "gy", "gz", None, None), P("gx", "gy", "gz", None)),
        check_vma=False,
    )
```
